128 devices in a mesh: cap: 4 (over y), lat: 16 (over x, z), rad: 2 (over core).
Axes of the slice: x: 4, y: 4, z: 4, core: 2. Of those that a mesh axis runs over, the one named last changes fastest.
Arguments:
- forcing: float32 [64, 4096, 256], P('cap', 'lat', 'rad'), may hold values from -6 to 6
- viscosity: float32 [64, 4096, 256], P('cap', 'lat', 'rad'), may hold values from 0.001 to 1000
- harmonic_basis: bfloat16 [4096, 4096], replicated, may hold values from -0.09375 to 0.09375
- damping_weights: float32 [4096], replicated, may hold values from 0.1 to 1
- unit_plates: int32 [64, 512, 1], P(('cap', 'lat')), may hold values from 0 to 127; in each aligned block of 512 rows (0 to 511, 512 to 1023, ..., all dimensions but the last counted through in order) at most 8 rows name the same one
Outputs:
- flow_costate: float32 [64, 4096, 256], P('cap', 'lat', 'rad')
- thermal_costate: float32 [64, 4096, 256], P('cap', 'lat', 'rad')
- tectonic_sensitivity: float32 [128, 2, 1024], P(('cap', 'lat', 'rad'))
The draws below stay inside these ranges and needn't reach their ends.
Inputs may be any that keep to these rules, and one draw needn't show every extreme that they name: `unit_plates`: among the 512 units of one tile no plate-mesh block is named more than 8 times, and in every draw some tile names one block exactly 8 times.
All inputs are finite; a program needn't handle non-finite values.
Results may differ from the reference program's by a relative error of at most 0.0019.
Values may be sent and summed in bfloat16 or wider, within the bound.
A program may use at most 128 MiB of HBM per device.

```python
import math
import jax
import jax.numpy as jnp
import numpy as np
from jax import lax

CX = 16
CY = 256
CZ = 128
CB = 8
ITERS = 2
ALONG_X_COUNT = 64
ALONG_Y_COUNT = 4096
DEPTH_COUNT = 256
TILES = 64
UNITS = 512
PLATES = 128
MOST = 8
N_CAP = 4
N_LAT = 16
N_RAD = 2


def block_scale(own_key, extent, shards, smallest, high):
    def one(dim, blocks):
        draws = jax.random.uniform(jax.random.fold_in(jax.random.fold_in(own_key, 6), dim), (blocks,), jnp.float32, smallest / len(shards), high / len(shards))
        return jnp.repeat(jnp.exp(draws), extent[dim] // blocks).reshape((-1,) + (1,) * (len(extent) - dim - 1))

    factor_of = one(*shards[0])
    for cut in shards[1:]:
        factor_of = factor_of * one(*cut)
    return factor_of


def shared_out(key, own, number, rows, amount, top, bound, skew):
    ranking = jax.random.permutation(key, amount)
    heavy_load, common = shares(amount, rows * top, bound, skew, True), shares(amount, rows * top, bound, skew, False)
    places = jnp.arange(amount)

    def named(sizes, offset_by):
        used = int((sizes > 0).sum())
        fixed = max(1, used // 4)
        shifted = fixed + (places - fixed + offset_by * (used - fixed)) % max(1, amount - fixed)
        return jnp.zeros((amount,), jnp.int32).at[ranking[jnp.where(places < fixed, places, shifted)]].set(jnp.asarray(sizes, jnp.int32))

    sizes = jnp.where(number % 4 == 0, named(heavy_load, number // 4), named(common, number - number // 4 - 1))
    mixed = jax.random.permutation(jax.random.fold_in(own, 3), amount)
    giver, receiver = mixed[0:amount // 2 * 2:2], mixed[1:amount // 2 * 2:2]
    room = jnp.minimum(sizes[giver] - 1, bound - sizes[receiver]) // 2
    room = jnp.where((giver == ranking[0]) | (receiver == ranking[0]) | (sizes[receiver] == 0), 0, jnp.maximum(room, 0))
    shifted = jax.random.randint(jax.random.fold_in(own, 4), (amount // 2,), 0, 1 << 20) % (room + 1)
    sizes = sizes.at[giver].add(-shifted).at[receiver].add(shifted)
    items = jnp.searchsorted(jnp.cumsum(sizes), jnp.arange(rows * top), side="right").astype(jnp.int32)
    grid = items.reshape(top, rows).T
    grid = grid[jax.random.permutation(jax.random.fold_in(own, 1), rows)]
    offset_by = jax.random.randint(jax.random.fold_in(own, 2), (rows, 1), 0, top)
    return jnp.take_along_axis(grid, (jnp.arange(top)[None, :] + offset_by) % top, axis=1)


def shares(number_of, total, bound, slope, full):
    portions = [(1 << 20) // math.isqrt(rank ** slope) + 1 for rank in range(1, number_of + 1)]
    largest = bound if full else min(bound, max(-(-total // number_of), total * portions[0] // sum(portions)))
    least = 1 if total - largest >= number_of - 1 else 0
    counts, surplus = [largest] + [least] * (number_of - 1), total - largest - least * (number_of - 1)
    while surplus > 0:
        free = [i for i in range(1, number_of) if counts[i] < largest] or [i for i in range(1, number_of) if counts[i] < bound]
        whole, remaining = sum([portions[i] for i in free]), surplus
        for i in free:
            addition = min(bound - counts[i], max(1, remaining * portions[i] // whole), surplus)
            counts[i] = counts[i] + addition
            surplus = surplus - addition
    return np.array(counts)


def gaussian(key, dims, scale, bound, split=(), kind=jnp.bfloat16):
    result = jax.random.normal(key, dims, jnp.float32) * scale
    if len(split) > 0:
        result = block_scale(key, dims, split, -0.22, 0.18) * result
    return jnp.clip(result, min=-bound, max=bound).astype(kind)


def setup_inputs(seed: int = 0) -> dict:
    streams_of = jax.random.split(jax.random.key(seed), 6)
    forcing = gaussian(streams_of[0], (ALONG_X_COUNT, ALONG_Y_COUNT, DEPTH_COUNT), 1.0, 6.0, ((0, 4), (1, 16), (2, 2)), jnp.float32)
    viscosity = jnp.clip(jnp.exp(math.log(1000.0) - 13.815511 * jax.random.uniform(streams_of[1], (ALONG_X_COUNT, ALONG_Y_COUNT, DEPTH_COUNT), jnp.float32) ** block_scale(streams_of[1], (ALONG_X_COUNT, ALONG_Y_COUNT, DEPTH_COUNT), ((0, 4), (1, 16), (2, 2)), -0.2, 0.2)), 0.001, 1000.0)
    harmonic_basis = gaussian(streams_of[2], (ALONG_Y_COUNT, ALONG_Y_COUNT), ALONG_Y_COUNT ** -0.5, 0.09375)
    damping_weights = jnp.clip(jnp.exp(jax.random.uniform(streams_of[3], (ALONG_Y_COUNT,), jnp.float32, math.log(0.1), math.log(1.0))), 0.1, 1.0)
    unit_plates_keys = jax.random.split(jax.random.fold_in(streams_of[4], 1), TILES * UNITS // UNITS)
    unit_plates_turns = jax.random.permutation(jax.random.fold_in(streams_of[4], 3), TILES * UNITS // UNITS)
    unit_plates = jax.vmap(lambda own, number: shared_out(jax.random.fold_in(streams_of[4], 2), own, number, UNITS, PLATES, 1, MOST, 2))(unit_plates_keys, unit_plates_turns).reshape((TILES, UNITS, 1))
    return {"forcing": forcing, "viscosity": viscosity, "harmonic_basis": harmonic_basis, "damping_weights": damping_weights, "unit_plates": unit_plates}


mass_term = 1.0


def neighbours(padded):
    return [padded[2:, 1:-1, 1:-1], padded[:-2, 1:-1, 1:-1],
            padded[1:-1, 2:, 1:-1], padded[1:-1, :-2, 1:-1],
            padded[1:-1, 1:-1, 2:], padded[1:-1, 1:-1, :-2]]


def reference(forcing, viscosity, harmonic_basis, damping_weights, unit_plates):
    face_coeffs = [0.5 * (viscosity + other) for other in neighbours(jnp.pad(viscosity, 1))]

    def operate(field):
        result_field = mass_term * field
        for face_coeff, neighbour in zip(face_coeffs, neighbours(jnp.pad(field, 1))):
            result_field = result_field + face_coeff * (field - neighbour)
        return result_field

    flow_costate = jnp.zeros_like(forcing)
    residual = forcing
    direction = forcing
    norm_now = jnp.sum(residual * residual)
    for iteration in range(ITERS):
        image = operate(direction)
        step_size = norm_now / jnp.sum(direction * image)
        flow_costate = flow_costate + step_size * direction
        residual = residual - step_size * image
        norm_next = jnp.sum(residual * residual)
        direction = residual + (norm_next / norm_now) * direction
        norm_now = norm_next

    rounded = lax.optimization_barrier(flow_costate.astype(jnp.bfloat16)).astype(jnp.float32)
    flat_field = rounded.transpose(1, 0, 2).reshape(ALONG_Y_COUNT, ALONG_X_COUNT * DEPTH_COUNT)
    basis_wide = harmonic_basis.astype(jnp.float32)
    harmonic_coef = jnp.dot(basis_wide, flat_field, precision=lax.Precision.HIGHEST, preferred_element_type=jnp.float32)
    scaled = lax.optimization_barrier((damping_weights[:, None] * harmonic_coef).astype(jnp.bfloat16)).astype(jnp.float32)
    spectral_filtering = jnp.dot(basis_wide.T, scaled, precision=lax.Precision.HIGHEST, preferred_element_type=jnp.float32)
    thermal_costate = flow_costate + spectral_filtering.reshape(ALONG_Y_COUNT, ALONG_X_COUNT, DEPTH_COUNT).transpose(1, 0, 2)

    weighted = viscosity * flow_costate
    unit_rows = weighted.reshape(N_CAP, CX, N_LAT, CY // CB, CB, N_RAD, CZ)
    unit_rows = unit_rows.transpose(0, 2, 5, 1, 3, 4, 6).reshape(TILES, N_RAD, UNITS, CB * CZ)
    plate_list = unit_plates[:, :, 0]
    match_table = (plate_list[:, :, None] == jnp.arange(PLATES, dtype=jnp.int32)[None, None, :]).astype(jnp.float32)
    tectonic_sensitivity = jnp.einsum('tup,truf->prf', match_table, unit_rows, precision=lax.Precision.HIGHEST)
    return flow_costate, thermal_costate, tectonic_sensitivity
```

```python
import jax
import jax.numpy as jnp
from jax import lax
from jax.experimental import pallas as pl
from jax.experimental.pallas import tpu as pltpu
from jax.sharding import PartitionSpec as P

MESH = pl.DeviceIdType.MESH
F32 = jnp.float32
BF16 = jnp.bfloat16
CX, CY, CZ = 16, 256, 128
NY = 4096
RB = 64
NB = CY // RB
NLAT, NCAP, NRAD = 16, 4, 2
HALF = NY // 2


def iota(shape, dim):
    return lax.broadcasted_iota(jnp.int32, shape, dim)


def fold(x):
    return jnp.sum(x.reshape(x.shape[0] // 8, 8, CZ), axis=0)


def kernel(b_hbm, v_hbm, basis_hbm, damp_ref, plates_ref, flow_hbm, back_hbm, tect_ref,
           bp, vp, wv, flow, fb, basis, xm, xo, coef, st, outb,
           pb, pv, pw, qb, qv, qw, wx, wy, part, recv_a, acc_a, recv_b, acc_b, recv_c,
           ar1, ar2, arv,
           loc_sem, basis_sem, out_sem, hs, hr, s1s, s1r, s2s, s2r,
           as_, ar_, fs, fr, ss, sr, rs, rr, pas, par, pbs, pbr, pcs, pcr):
    cap = lax.axis_index("cap")
    lat = lax.axis_index("lat")
    rad = lax.axis_index("rad")
    mx = lat // 4
    mz = lax.rem(lat, 4)
    up_cap, dn_cap = lax.rem(cap + 1, NCAP), lax.rem(cap + NCAP - 1, NCAP)
    up_lat, dn_lat = lax.rem(lat + 1, NLAT), lax.rem(lat + NLAT - 1, NLAT)
    sib = 1 - rad

    loads = [
        pltpu.make_async_copy(b_hbm, bp.at[1:17, 8:264, :], loc_sem.at[0]),
        pltpu.make_async_copy(v_hbm, vp.at[1:17, 8:264, :], loc_sem.at[1]),
    ]
    for cp in loads:
        cp.start()
    basis_cp = pltpu.make_async_copy(basis_hbm, basis, basis_sem)
    basis_cp.start()

    bar = pltpu.get_barrier_semaphore()
    for k in range(1, NLAT):
        pl.semaphore_signal(bar, inc=1, device_id={"lat": lax.rem(lat + k, NLAT)}, device_id_type=MESH)
    for k in range(1, 8):
        pl.semaphore_signal(
            bar, inc=1,
            device_id={"cap": lax.rem(cap + k // 2, NCAP), "rad": lax.rem(rad + k % 2, NRAD)},
            device_id_type=MESH)
    pl.semaphore_wait(bar, 22)

    def rcopy(src, dst, ssem, rsem, **dev):
        return pltpu.make_async_remote_copy(
            src_ref=src, dst_ref=dst, send_sem=ssem, recv_sem=rsem, device_id=dev, device_id_type=MESH)

    yh, xh = [], []
    for q, (hbm, pad) in enumerate(((b_hbm, bp), (v_hbm, vp))):
        yh.append(rcopy(hbm.at[:, 248:256, :], pad.at[1:17, 0:8, :], hs.at[q], hr.at[q], lat=up_lat))
        yh.append(rcopy(hbm.at[:, 0:8, :], pad.at[1:17, 264:272, :], hs.at[2 + q], hr.at[2 + q], lat=dn_lat))
        xh.append(rcopy(hbm.at[15], pad.at[0, 8:264, :], hs.at[4 + q], hr.at[4 + q], cap=up_cap))
        xh.append(rcopy(hbm.at[0], pad.at[17, 8:264, :], hs.at[6 + q], hr.at[6 + q], cap=dn_cap))
    for cp in xh + yh:
        cp.start()
    for cp in loads:
        cp.wait()

    lane = iota((RB, CZ), 1)
    inner = jnp.where(rad == 0, CZ - 1, 0)
    outer = jnp.where(rad == 0, 0, CZ - 1)

    def pack(ref, base, row0, dst):
        for yb in range(NB):
            rows = slice(row0 + yb * RB, row0 + (yb + 1) * RB)
            acc = jnp.zeros((RB, CZ), F32)
            for x in range(CX):
                moved = pltpu.roll(ref[base + x, rows, :], x + 1 - rad, 1)
                acc = jnp.where(lane == x, moved, acc)
            dst[yb * RB:(yb + 1) * RB, :] = acc

    pack(bp, 1, 8, pb)
    zb = rcopy(pb, qb, hs.at[8], hr.at[8], rad=sib)
    zb.start()
    pack(vp, 1, 8, pv)
    zv = rcopy(pv, qv, hs.at[9], hr.at[9], rad=sib)
    zv.start()

    for cp in yh:
        cp.wait()
    for edge, rows in ((0, slice(0, 8)), (NLAT - 1, slice(264, 272))):
        @pl.when(lat == edge)
        def _():
            bp[1:17, rows, :] = jnp.zeros((CX, 8, CZ), F32)
            vp[1:17, rows, :] = jnp.zeros((CX, 8, CZ), F32)
    zb.wait()
    zv.wait()
    qb[...] = (pv[...] + qv[...]) * (pb[...] - qb[...])

    def plane(X, sums):
        m0, n1, n2 = sums
        shift = lax.rem(CZ - X + rad, CZ)
        for yb in range(NB):
            y0 = 8 + yb * RB
            rows = slice(y0, y0 + RB)
            b0, v0 = bp[X, rows, :], vp[X, rows, :]
            acc = (v0 + vp[X + 1, rows, :]) * (b0 - bp[X + 1, rows, :])
            acc += (v0 + vp[X - 1, rows, :]) * (b0 - bp[X - 1, rows, :])
            for d in (-1, 1):
                near = slice(y0 + d, y0 + d + RB)
                acc += (v0 + vp[X, near, :]) * (b0 - bp[X, near, :])
            br, vr = pltpu.roll(b0, CZ - 1, 1), pltpu.roll(v0, CZ - 1, 1)
            flux = jnp.where(lane < CZ - 1, (v0 + vr) * (b0 - br), 0.0)
            acc += flux - pltpu.roll(flux, 1, 1)
            acc += jnp.where(lane == outer, v0 * b0, 0.0)
            acc += jnp.where(lane == inner, pltpu.roll(qb[yb * RB:(yb + 1) * RB, :], shift, 1), 0.0)
            w = 0.5 * acc
            wv[X - 1, yb * RB:(yb + 1) * RB, :] = w
            m0 += fold(b0 * b0)
            n1 += fold(b0 * w)
            n2 += fold(w * w)
        return m0, n1, n2

    zero = jnp.zeros((8, CZ), F32)
    sums = lax.fori_loop(2, 16, plane, (zero, zero, zero))
    for cp in xh:
        cp.wait()
    for edge, at in ((0, 0), (NCAP - 1, 17)):
        @pl.when(cap == edge)
        def _():
            bp[at] = jnp.zeros((272, CZ), F32)
            vp[at] = jnp.zeros((272, CZ), F32)
    sums = plane(1, sums)
    sums = plane(16, sums)
    m0, n1, n2 = sums

    wxc = rcopy(wv.at[0], wx, hs.at[10], hr.at[10], cap=dn_cap)
    wxc.start()
    wyc = rcopy(wv.at[:, 0:8, :], wy, hs.at[11], hr.at[11], lat=dn_lat)
    wyc.start()
    pack(wv, 0, 0, pw)
    wzc = rcopy(pw, qw, hs.at[12], hr.at[12], rad=sib)
    wzc.start()

    row = iota((RB, CZ), 0)

    def energy(x, n3, with_x):
        for yb in range(NB):
            rows = slice(yb * RB, (yb + 1) * RB)
            prow = slice(8 + yb * RB, 8 + (yb + 1) * RB)
            w0, v0 = wv[x, rows, :], vp[x + 1, prow, :]
            acc = jnp.where(lane == outer, v0 * w0 * w0, 0.0)
            if with_x:
                d = w0 - wv[x + 1, rows, :]
                acc += (v0 + vp[x + 2, prow, :]) * (d * d)
            vu = vp[x + 1, 9 + yb * RB:9 + (yb + 1) * RB, :]
            if yb < NB - 1:
                d = w0 - wv[x, yb * RB + 1:(yb + 1) * RB + 1, :]
                acc += (v0 + vu) * (d * d)
            else:
                d = w0 - pltpu.roll(w0, RB - 1, 0)
                acc += jnp.where(row < RB - 1, (v0 + vu) * (d * d), 0.0)
            d = w0 - pltpu.roll(w0, CZ - 1, 1)
            acc += jnp.where(lane < CZ - 1, (v0 + pltpu.roll(v0, CZ - 1, 1)) * (d * d), 0.0)
            n3 += fold(acc)
        return n3

    n3 = lax.fori_loop(0, 15, lambda x, s: energy(x, s, True), zero)
    n3 = energy(15, n3, False)
    lower = jnp.where(cap == 0, 1.0, 0.0).astype(F32)
    w0 = wv[0]
    n3 += lower * fold(vp[1, 8:264, :] * w0 * w0)
    wlow = wv[:, 0:1, :]
    lower_y = jnp.where(lat == 0, 1.0, 0.0).astype(F32)
    edge_row = lower_y * jnp.sum(vp[1:17, 8:9, :] * wlow * wlow, axis=0)
    wzc.wait()
    d = pw[...] - qw[...]
    n3 += fold(0.5 * (pv[...] + qv[...]) * (d * d))
    wyc.wait()
    keep_y = jnp.where(lat == NLAT - 1, 0.0, 1.0).astype(F32)
    d = wv[:, 255:256, :] - keep_y * wy[:, 0:1, :]
    edge_row += jnp.sum((vp[1:17, 263:264, :] + vp[1:17, 264:265, :]) * (d * d), axis=0)
    wxc.wait()
    keep_x = jnp.where(cap == NCAP - 1, 0.0, 1.0).astype(F32)
    d = wv[15] - keep_x * wx[...]
    n3 += fold((vp[16, 8:264, :] + vp[17, 8:264, :]) * (d * d))

    r8 = iota((8, CZ), 0)
    total = jnp.where(r8 == 0, jnp.sum(m0, axis=0, keepdims=True), 0.0)
    total = jnp.where(r8 == 1, jnp.sum(n1, axis=0, keepdims=True), total)
    total = jnp.where(r8 == 2, jnp.sum(n2, axis=0, keepdims=True), total)
    total = jnp.where(r8 == 3, 0.5 * (jnp.sum(n3, axis=0, keepdims=True) + edge_row), total)
    arv[0] = total
    ar1[lat] = total
    sends = []
    for k in range(1, NLAT):
        peer = lax.rem(lat + k, NLAT)
        cp = rcopy(arv.at[0], ar1.at[lat], s1s.at[k], s1r.at[k], lat=peer)
        cp.start()
        sends.append(cp)
    for cp in sends:
        cp.wait()
    total = jnp.sum(ar1[...], axis=0)
    arv[1] = total
    ar2[cap * 2 + rad] = total
    sends = []
    for k in range(1, 8):
        pc, pr = lax.rem(cap + k // 2, NCAP), lax.rem(rad + k % 2, NRAD)
        cp = rcopy(arv.at[1], ar2.at[cap * 2 + rad], s2s.at[k], s2r.at[k], cap=pc, rad=pr)
        cp.start()
        sends.append(cp)
    for cp in sends:
        cp.wait()
    sums = jnp.sum(jnp.sum(ar2[...], axis=0), axis=1, keepdims=True)
    t0 = sums[0:1]
    e1, e2, e3 = sums[1:2] / t0, sums[2:3] / t0, sums[3:4] / t0
    step0 = 1.0 / (1.0 + e1)
    ratio = jnp.maximum((e2 - e1 * e1) * step0 * step0, 0.0)
    g, h = (1.0 - step0) + ratio, -step0
    pap = g * g * (1.0 + e1) + 2.0 * g * h * (e1 + e2) + h * h * (e2 + e3)
    step1 = ratio / jnp.maximum(jnp.maximum(pap, ratio), 1e-30)
    alpha, beta = step0 + step1 * g, step1 * h

    def offset(k):
        return lax.rem(mx + k // 4, 4) * 4 + lax.rem(mz + lax.rem(k, 4), 4)

    def solve(x):
        f = alpha * bp[x + 1, 8:264, :] + beta * wv[x]
        flow[x] = f
        fb[x] = f.astype(BF16)

    solve(lat)
    xm[lat] = fb[lat]

    @pl.loop(1, NLAT)
    def _(k):
        dest = offset(k)
        solve(dest)
        rcopy(fb.at[dest], xm.at[lat], as_.at[k], ar_.at[k], lat=dest).start()

    flow_cp = pltpu.make_async_copy(flow, flow_hbm, out_sem.at[0])
    flow_cp.start()

    def forward(src):
        return rcopy(xm.at[src], xo.at[src], fs.at[src], fr.at[src], rad=sib)

    def source(k):
        return lax.rem(mx + 4 - k // 4, 4) * 4 + lax.rem(mz + 4 - k % 4, 4)

    forward(lat).start()

    @pl.loop(0, CX)
    def _(x):
        wv[x] = vp[x + 1, 8:264, :] * flow[x]
    plate_row = iota((128, 128), 0)
    hots = [jnp.where(plates_ref[q:q + 1, :] == plate_row, 1.0, 0.0).astype(BF16) for q in range(4)]
    hot = jnp.concatenate(hots, axis=1)
    flat = wv.reshape(CX * CY, CZ)
    pflat = part.reshape(128 * 8, CZ)
    for j in range(8):
        u = flat[pl.ds(j, 512, stride=8), :]
        hi = u.astype(BF16)
        lo = (u - hi.astype(F32)).astype(BF16)
        pflat[pl.ds(j, 128, stride=8), :] = (
            jnp.dot(hot, hi, preferred_element_type=F32) + jnp.dot(hot, lo, preferred_element_type=F32))
    stage_a = []
    for k in range(1, NCAP):
        to = lax.rem(cap + k, NCAP)
        cp = rcopy(part.at[pl.ds(to * 32, 32)], recv_a.at[k], pas.at[k], par.at[k], cap=to)
        cp.start()
        stage_a.append(cp)

    basis_cp.wait()
    krow = rad * HALF
    for g4 in range(4):
        srcs = [source(g4 * 4 + q) for q in range(4)]
        for q, src in enumerate(srcs):
            if g4 or q:
                k = g4 * 4 + q
                rcopy(fb.at[src], xm.at[src], as_.at[k], ar_.at[k], lat=src).wait_recv()
                forward(src).start()
        for src in srcs:
            forward(src).wait_recv()
        gx = lax.rem(mx + 4 - g4, 4)
        cols = pl.ds(pl.multiple_of(gx * 1024, 1024), 1024)
        xs = jnp.concatenate(
            [xm[pl.ds(gx * 4, 4)].reshape(1024, CZ), xo[pl.ds(gx * 4, 4)].reshape(1024, CZ)], axis=1)

        @pl.loop(0, 2)
        def _(i):
            rows = pl.ds(pl.multiple_of(krow + i * 1024, 1024), 1024)
            prod = jnp.dot(basis[rows, cols], xs, preferred_element_type=F32)
            crow = pl.ds(pl.multiple_of(i * 1024, 1024), 1024)
            if g4 == 0:
                coef[crow, :] = prod
            else:
                coef[crow, :] += prod

    kcols = pl.ds(pl.multiple_of(rad * HALF, HALF), HALF)
    dw = damp_ref[:, kcols]
    st[1, :, kcols] = (coef[:, CZ:].T * dw).astype(BF16)
    swap = rcopy(st.at[1, :, kcols], st.at[0, :, kcols], ss, sr, rad=sib)
    swap.start()
    st[0, :, kcols] = (coef[:, :CZ].T * dw).astype(BF16)

    for cp in stage_a:
        cp.wait()
    acc_a[...] = (part[pl.ds(cap * 32, 32)] + recv_a[1] + recv_a[2] + recv_a[3])
    recv_b[lat] = acc_a[pl.ds(lat * 2, 2)]
    stage_b = []
    for k in range(1, NLAT):
        to = lax.rem(lat + k, NLAT)
        cp = rcopy(acc_a.at[pl.ds(to * 2, 2)], recv_b.at[lat], pbs.at[k], pbr.at[k], lat=to)
        cp.start()
        stage_b.append(cp)
    swap.wait()

    @pl.loop(0, 8)
    def _(i):
        tx = lax.rem(mx + 1 + i // 2, 4)
        first = tx * 4 + lax.rem(i, 2) * 2
        cols = pl.ds(pl.multiple_of(first * CY, 512), 512)
        res = jnp.dot(st[0], basis[:, cols], preferred_element_type=F32)
        outb[pl.ds(first, 2)] = res.T.astype(BF16).reshape(2, CY, CZ)
        for q in range(2):
            dest = first + q

            @pl.when(dest != lat)
            def _():
                rcopy(outb.at[dest], back_hbm.at[lat], rs.at[dest], rr.at[lat], lat=dest).start()

    own = pltpu.make_async_copy(outb.at[lat], back_hbm.at[lat], out_sem.at[1])
    own.start()

    for cp in stage_b:
        cp.wait()
    acc_b[...] = jnp.sum(recv_b[...], axis=0)
    swap_c = rcopy(acc_b.at[sib], recv_c, pcs, pcr, rad=sib)
    swap_c.start()
    swap_c.wait()
    tect_ref[rad] = acc_b[rad]
    tect_ref[sib] = recv_c[...]

    own.wait()
    flow_cp.wait()
    for k in range(1, NLAT):
        dest = offset(k)
        rcopy(fb.at[dest], xm.at[lat], as_.at[k], ar_.at[k], lat=dest).wait_send()
    for src in range(NLAT):
        forward(src).wait_send()

    @pl.loop(0, NLAT)
    def _(dest):
        @pl.when(dest != lat)
        def _():
            cp = rcopy(outb.at[dest], back_hbm.at[dest], rs.at[dest], rr.at[dest], lat=dest)
            cp.wait_send()
            cp.wait_recv()


def body(forcing, viscosity, harmonic_basis, damping_weights, unit_plates):
    DMA = pltpu.SemaphoreType.DMA
    vm = pltpu.VMEM
    anys = pl.BlockSpec(memory_space=pl.ANY)
    vmem = pl.BlockSpec(memory_space=pltpu.VMEM)
    block = (CX, CY, CZ)
    flow, back, tect = pl.pallas_call(
        kernel,
        out_shape=(
            jax.ShapeDtypeStruct(block, F32),
            jax.ShapeDtypeStruct(block, BF16),
            jax.ShapeDtypeStruct((2, 8, CZ), F32),
        ),
        in_specs=[anys, anys, anys, vmem, vmem],
        out_specs=(anys, anys, vmem),
        scratch_shapes=[
            vm((18, 272, CZ), F32), vm((18, 272, CZ), F32), vm(block, F32), vm(block, F32), vm(block, BF16),
            vm((NY, NY), BF16), vm(block, BF16), vm(block, BF16), vm((HALF, 256), F32),
            vm((2, CZ, NY), BF16), vm(block, BF16),
            vm((CY, CZ), F32), vm((CY, CZ), F32), vm((CY, CZ), F32),
            vm((CY, CZ), F32), vm((CY, CZ), F32), vm((CY, CZ), F32),
            vm((CY, CZ), F32), vm((CX, 8, CZ), F32),
            vm((128, 8, CZ), F32), vm((4, 32, 8, CZ), F32), vm((32, 8, CZ), F32),
            vm((NLAT, 2, 8, CZ), F32), vm((2, 8, CZ), F32), vm((8, CZ), F32),
            vm((NLAT, 8, CZ), F32), vm((8, 8, CZ), F32), vm((2, 8, CZ), F32),
            DMA((2,)), DMA, DMA((2,)), DMA((13,)), DMA((13,)),
            DMA((16,)), DMA((16,)), DMA((8,)), DMA((8,)),
            DMA((16,)), DMA((16,)), DMA((16,)), DMA((16,)), DMA, DMA, DMA((16,)), DMA((16,)),
            DMA((4,)), DMA((4,)), DMA((16,)), DMA((16,)), DMA, DMA,
        ],
        compiler_params=pltpu.CompilerParams(
            vmem_limit_bytes=60 << 20, collective_id=0, has_side_effects=True),
        name="adjoint",
    )(forcing, viscosity, harmonic_basis, damping_weights.reshape(1, NY), unit_plates.reshape(4, 128))
    thermal = flow + back.astype(F32)
    return flow, thermal, tect.reshape(1, 2, 8 * CZ)


def solution(mesh):
    in_specs = (
        P("cap", "lat", "rad"),
        P("cap", "lat", "rad"),
        P(),
        P(),
        P(("cap", "lat"), None, None),
    )
    out_specs = (
        P("cap", "lat", "rad"),
        P("cap", "lat", "rad"),
        P(("cap", "lat", "rad"), None, None),
    )
    return jax.shard_map(body, mesh=mesh, in_specs=in_specs, out_specs=out_specs, check_vma=False)
```

```python
import jax
import jax.numpy as jnp
from jax import lax
from jax.experimental import pallas as pl
from jax.experimental.pallas import tpu as pltpu
from jax.sharding import PartitionSpec as P

MESH = pl.DeviceIdType.MESH
F32 = jnp.float32
BF16 = jnp.bfloat16
CX, CY, CZ = 16, 256, 128
NY = 4096
RB = 64
NB = CY // RB
NLAT, NCAP, NRAD = 16, 4, 2
HALF = NY // 2


def iota(shape, dim):
    return lax.broadcasted_iota(jnp.int32, shape, dim)


def fold(x):
    return jnp.sum(x.reshape(x.shape[0] // 8, 8, CZ), axis=0)


def kernel(b_hbm, v_hbm, basis_hbm, damp_ref, plates_ref, flow, uv, tect_ref,
           bp, vp, fb, basis, xm, xo, coef, st, outb, rec,
           pb, pv, pu, qb, qv, qu, ybm, ybp, yvm, yvp, yu, xup, xdn,
           part, recv_a, acc_a, recv_b, acc_b, recv_c, mine, rows,
           loc_sem, basis_sem, deep, hs, hr, g_send, g_recv,
           as_, ar_, fs, fr, ss, sr, rs, rr, pas, par, pbs, pbr, pcs, pcr):
    cap = lax.axis_index("cap")
    lat = lax.axis_index("lat")
    rad = lax.axis_index("rad")
    mx = lat // 4
    mz = lax.rem(lat, 4)
    up_cap, dn_cap = lax.rem(cap + 1, NCAP), lax.rem(cap + NCAP - 1, NCAP)
    up_lat, dn_lat = lax.rem(lat + 1, NLAT), lax.rem(lat + NLAT - 1, NLAT)
    sib = 1 - rad

    loads = [
        pltpu.make_async_copy(b_hbm, bp.at[1:17], loc_sem.at[0]),
        pltpu.make_async_copy(v_hbm, vp.at[1:17], loc_sem.at[1]),
    ]
    for cp in loads:
        cp.start()

    bar = pltpu.get_barrier_semaphore()
    column = [(k // 2, k % 2) for k in range(1, 8)]

    def tell(sem, **dev):
        pl.semaphore_signal(sem, inc=1, device_id=dev, device_id_type=MESH)

    def fellow(k):
        return {"cap": lax.rem(cap + k[0], NCAP), "rad": lax.rem(rad + k[1], NRAD)}

    for k in column:
        tell(bar, **fellow(k))
    for k in range(1, NLAT):
        tell(bar, lat=lax.rem(lat + k, NLAT))
    pl.semaphore_wait(bar, 22)

    def rcopy(src, dst, ssem, rsem, **dev):
        return pltpu.make_async_remote_copy(
            src_ref=src, dst_ref=dst, send_sem=ssem, recv_sem=rsem, device_id=dev, device_id_type=MESH)

    yh, xh = [], []
    for q, (hbm, pad, lo, hi) in enumerate(((b_hbm, bp, ybm, ybp), (v_hbm, vp, yvm, yvp))):
        yh.append(rcopy(hbm.at[:, 248:256, :], lo, hs.at[q], hr.at[q], lat=up_lat))
        yh.append(rcopy(hbm.at[:, 0:8, :], hi, hs.at[2 + q], hr.at[2 + q], lat=dn_lat))
        xh.append(rcopy(hbm.at[15], pad.at[0], hs.at[4 + q], hr.at[4 + q], cap=up_cap))
        xh.append(rcopy(hbm.at[0], pad.at[17], hs.at[6 + q], hr.at[6 + q], cap=dn_cap))
    for cp in xh + yh:
        cp.start()
    for cp in loads:
        cp.wait()
    lane = iota((RB, CZ), 1)
    row = iota((RB, CZ), 0)
    edge = (lane == 0) | (lane == CZ - 1)

    def pack(ref, base, dst):
        for yb in range(NB):
            rows_ = slice(yb * RB, (yb + 1) * RB)
            acc = jnp.zeros((RB, CZ), F32)
            for x in range(CX):
                acc = jnp.where(lane // 2 == x, pltpu.roll(ref[base + x, rows_, :], 2 * x + 1, 1), acc)
            dst[rows_, :] = acc

    wide = iota((CY, CZ), 1)
    facing = lax.rem(wide, 2) == rad

    def across(q):
        turned = jnp.where(rad == 0, pltpu.roll(q, CZ - 1, 1), pltpu.roll(q, 1, 1))
        return jnp.where(facing, turned, 0.0)

    pack(bp, 1, pb)
    zb = rcopy(pb, qb, hs.at[8], hr.at[8], rad=sib)
    zb.start()
    pack(vp, 1, pv)
    zv = rcopy(pv, qv, hs.at[9], hr.at[9], rad=sib)
    zv.start()
    for k in column:
        tell(deep, **fellow(k))
    basis_cp = pltpu.make_async_copy(basis_hbm, basis, basis_sem)
    basis_cp.start()
    zero = jnp.zeros((8, CZ), F32)

    def square(x, s):
        b0 = bp[x]
        return s + fold(b0 * b0)

    m0 = lax.fori_loop(1, 17, square, zero)
    zb.wait()
    zv.wait()
    qv[...] = pv[...] + across(qv[...])
    qb[...] = qv[...] * (pb[...] - across(qb[...]))

    def plane(X, carry):
        shift = CZ + 1 - 2 * X
        for yb in range(NB):
            y0 = yb * RB
            rows_ = slice(y0, y0 + RB)
            b0, v0 = bp[X, rows_, :], vp[X, rows_, :]
            acc = (v0 + vp[X + 1, rows_, :]) * (b0 - bp[X + 1, rows_, :])
            acc += (v0 + vp[X - 1, rows_, :]) * (b0 - bp[X - 1, rows_, :])
            if yb > 0:
                near = slice(y0 - 1, y0 - 1 + RB)
                acc += (v0 + vp[X, near, :]) * (b0 - bp[X, near, :])
            else:
                flux = (v0 + pltpu.roll(v0, 1, 0)) * (b0 - pltpu.roll(b0, 1, 0))
                acc += jnp.where(row > 0, flux, 0.0)
            if yb < NB - 1:
                near = slice(y0 + 1, y0 + 1 + RB)
                acc += (v0 + vp[X, near, :]) * (b0 - bp[X, near, :])
            else:
                flux = (v0 + pltpu.roll(v0, RB - 1, 0)) * (b0 - pltpu.roll(b0, RB - 1, 0))
                acc += jnp.where(row < RB - 1, flux, 0.0)
            flux = (v0 + pltpu.roll(v0, CZ - 1, 1)) * (b0 - pltpu.roll(b0, CZ - 1, 1))
            flux = jnp.where(lane < CZ - 1, flux, 0.0)
            acc += flux - pltpu.roll(flux, 1, 1)
            acc += jnp.where(edge, pltpu.roll(qb[rows_, :], shift, 1), 0.0)
            uv[X - 1, rows_, :] = acc
        return carry

    low_y = jnp.where(lat == 0, 0.0, 1.0).astype(F32)
    high_y = jnp.where(lat == NLAT - 1, 0.0, 1.0).astype(F32)

    def lat_faces(a, b):
        for at, bh, vh, far, keep in ((0, ybm, yvm, 7, low_y), (255, ybp, yvp, 0, high_y)):
            here = slice(at, at + 1)
            there = slice(far, far + 1)
            uv[a:b, here, :] += ((vp[a + 1:b + 1, here, :] + keep * vh[a:b, there, :])
                                 * (bp[a + 1:b + 1, here, :] - keep * bh[a:b, there, :]))

    def energy(x, sums, with_x):
        n1, n2, n3 = sums
        for yb in range(NB):
            y0 = yb * RB
            rows_ = slice(y0, y0 + RB)
            u0, v0, b0 = uv[x, rows_, :], vp[x + 1, rows_, :], bp[x + 1, rows_, :]
            d = u0 - pltpu.roll(u0, CZ - 1, 1)
            acc = jnp.where(lane < CZ - 1, (v0 + pltpu.roll(v0, CZ - 1, 1)) * (d * d), 0.0)
            if with_x:
                d = u0 - uv[x + 1, rows_, :]
                acc += (v0 + vp[x + 2, rows_, :]) * (d * d)
            if yb < NB - 1:
                near = slice(y0 + 1, y0 + 1 + RB)
                d = u0 - uv[x, near, :]
                acc += (v0 + vp[x + 1, near, :]) * (d * d)
            else:
                d = u0 - pltpu.roll(u0, RB - 1, 0)
                acc += jnp.where(row < RB - 1, (v0 + pltpu.roll(v0, RB - 1, 0)) * (d * d), 0.0)
            n1 += fold(b0 * u0)
            n2 += fold(u0 * u0)
            n3 += fold(acc)
        return n1, n2, n3

    lax.fori_loop(2, 16, plane, 0)
    for cp in yh:
        cp.wait()
    lat_faces(1, 15)
    sums = lax.fori_loop(1, 14, lambda x, s: energy(x, s, True), (zero, zero, zero))
    for cp in xh:
        cp.wait()
    for side, at in ((0, 0), (NCAP - 1, 17)):
        @pl.when(cap == side)
        def _():
            bp[at] = jnp.zeros((CY, CZ), F32)
            vp[at] = jnp.zeros((CY, CZ), F32)
    plane(1, 0)
    plane(16, 0)
    lat_faces(0, 1)
    lat_faces(15, 16)

    mid = CY // 2
    ux = [
        rcopy(uv.at[0, 0:mid], xup, hs.at[10], hr.at[10], cap=dn_cap),
        rcopy(uv.at[15, mid:CY], xdn, hs.at[11], hr.at[11], cap=up_cap),
    ]
    for cp in ux:
        cp.start()
    uy = rcopy(uv.at[:, 0:8, :], yu, hs.at[12], hr.at[12], lat=dn_lat)
    uy.start()
    pack(uv, 0, pu)
    uz = rcopy(pu, qu, hs.at[13], hr.at[13], rad=sib)
    uz.start()
    sums = energy(0, sums, True)
    sums = energy(14, sums, True)
    n1, n2, n3 = energy(15, sums, False)
    u0, u15 = uv[0, 0:mid], uv[15, mid:CY]
    first = jnp.where(cap == 0, 1.0, 0.0).astype(F32)
    last = jnp.where(cap == NCAP - 1, 1.0, 0.0).astype(F32)
    n3 += fold(first * vp[1, 0:mid] * (u0 * u0)) + fold(last * vp[16, mid:CY] * (u15 * u15))
    u0 = uv[:, 0:1, :]
    edge_row = jnp.sum((1.0 - low_y) * vp[1:17, 0:1, :] * (u0 * u0), axis=0)
    uz.wait()
    d = pu[...] - across(qu[...])
    n3 += fold(jnp.where(facing, 0.5, 1.0) * qv[...] * (d * d))
    uy.wait()
    d = uv[:, 255:256, :] - high_y * yu[:, 0:1, :]
    edge_row += jnp.sum((vp[1:17, 255:256, :] + high_y * yvp[:, 0:1, :]) * (d * d), axis=0)
    for cp in ux:
        cp.wait()
    d = uv[15, 0:mid] - (1.0 - last) * xup[...]
    n3 += fold((vp[16, 0:mid] + vp[17, 0:mid]) * (d * d))
    d = uv[0, mid:CY] - (1.0 - first) * xdn[...]
    n3 += fold((vp[1, mid:CY] + vp[0, mid:CY]) * (d * d))

    lane1 = iota((1, CZ), 1)
    line = jnp.zeros((1, CZ), F32)
    for q, s in enumerate((m0, n1, n2, n3)):
        s = jnp.sum(s, axis=0, keepdims=True)
        if q == 3:
            s = s + edge_row
        line = jnp.where(lane1 == q, jnp.sum(s, axis=1, keepdims=True), line)
    mine[...] = line
    place = (cap * NLAT + lat) * NRAD + rad
    rows[place] = line
    pl.semaphore_wait(deep, 7)
    ring = (0, 1, 2, 1)
    others = sorted(((c, x, z, r) for c in range(4) for x in range(4) for z in range(4) for r in range(2)),
                    key=lambda o: -(ring[o[0]] + ring[o[1]] + ring[o[2]]))
    for c, x, z, r in others:
        if (c, x, z, r) != (0, 0, 0, 0):
            rcopy(mine, rows.at[place], g_send, g_recv,
                  cap=lax.rem(cap + c, NCAP), lat=lax.rem(mx + x, 4) * 4 + lax.rem(mz + z, 4),
                  rad=lax.rem(rad + r, NRAD)).start()
    arrived = rows.at[pl.ds(0, 127)]
    pltpu.make_async_copy(arrived, arrived, g_recv).wait()
    tot = jnp.sum(rows[...], axis=0)
    t0, e1, e2, e3 = [jnp.sum(jnp.where(lane1 == q, tot, 0.0), axis=1, keepdims=True) for q in range(4)]
    e1, e2, e3 = 0.5 * e1 / t0, 0.25 * e2 / t0, 0.125 * e3 / t0
    step0 = 1.0 / (1.0 + e1)
    ratio = jnp.maximum((e2 - e1 * e1) * step0 * step0, 0.0)
    g, h = (1.0 - step0) + ratio, -step0
    pap = g * g * (1.0 + e1) + 2.0 * g * h * (e1 + e2) + h * h * (e2 + e3)
    step1 = ratio / jnp.maximum(jnp.maximum(pap, ratio), 1e-30)
    alpha, beta = step0 + step1 * g, 0.5 * step1 * h

    def away(dx, dz):
        return lax.rem(mx + dx, 4) * 4 + lax.rem(mz + dz, 4)

    def solve(x):
        f = alpha * bp[x + 1] + beta * uv[x]
        flow[x] = f
        fb[x] = f.astype(BF16)

    steps = [(1, 2), (3, 2), (1, 1), (3, 1), (1, 3), (3, 3), (1, 0), (3, 0), (2, 2), (0, 1), (2, 1), (0, 3), (2, 3), (0, 2), (2, 0)]

    def carry_out(dx, dz):
        dest = away(dx, dz)
        k = dx * 4 + dz
        return rcopy(fb.at[dest], xm.at[lat], as_.at[k], ar_.at[k], lat=dest)

    for dx, dz in steps:
        solve(away(dx, dz))
        carry_out(dx, dz).start()
    solve(lat)
    xm[lat] = fb[lat]

    def forward(src):
        return rcopy(xm.at[src], xo.at[src], fs.at[src], fr.at[src], rad=sib)

    forward(lat).start()

    @pl.loop(0, CX)
    def _(x):
        uv[x] = vp[x + 1] * flow[x]
    plate_row = iota((128, 128), 0)
    hots = [jnp.where(plates_ref[q:q + 1, :] == plate_row, 1.0, 0.0).astype(BF16) for q in range(4)]
    hot = jnp.concatenate(hots, axis=1)
    flat = uv.reshape(CX * CY, CZ)
    pflat = part.reshape(128 * 8, CZ)
    for j in range(8):
        u = flat[pl.ds(j, 512, stride=8), :]
        hi = u.astype(BF16)
        lo = (u - hi.astype(F32)).astype(BF16)
        pflat[pl.ds(j, 128, stride=8), :] = (
            jnp.dot(hot, hi, preferred_element_type=F32) + jnp.dot(hot, lo, preferred_element_type=F32))
    stage_a = []
    for k in range(1, NCAP):
        to = lax.rem(cap + k, NCAP)
        cp = rcopy(part.at[pl.ds(to * 32, 32)], recv_a.at[k], pas.at[k], par.at[k], cap=to)
        cp.start()
        stage_a.append(cp)

    basis_cp.wait()
    krow = rad * HALF
    swaps = []
    order = (1, 3, 0, 2)

    def block_of(g4):
        return lax.rem(mx + 4 - g4, 4)

    for step in range(5):
        if step < 4:
            g4 = order[step]
            for dz in (2, 1, 3, 0):
                if g4 or dz:
                    src = block_of(g4) * 4 + lax.rem(mz + 4 - dz, 4)
                    k = g4 * 4 + dz
                    rcopy(fb.at[src], xm.at[src], as_.at[k], ar_.at[k], lat=src).wait_recv()
                    forward(src).start()
        if step == 0:
            continue
        gx = block_of(order[step - 1])
        for q in range(4):
            forward(gx * 4 + q).wait_recv()
        cols = pl.ds(pl.multiple_of(gx * 1024, 1024), 1024)
        xs = jnp.concatenate(
            [xm[pl.ds(gx * 4, 4)].reshape(1024, CZ), xo[pl.ds(gx * 4, 4)].reshape(1024, CZ)], axis=1)
        for i in range(2):
            krows = pl.ds(pl.multiple_of(krow + i * 1024, 1024), 1024)
            crow = slice(i * 1024, (i + 1) * 1024)
            prod = jnp.dot(basis[krows, cols], xs, preferred_element_type=F32)
            if step == 1:
                coef[crow, :] = prod
            elif step < 4:
                coef[crow, :] += prod
            else:
                whole = coef[crow, :] + prod
                dw = damp_ref[:, krows]
                st[1, :, krows] = (whole[:, CZ:].T * dw).astype(BF16)
                swaps.append(rcopy(st.at[1, :, krows], st.at[0, :, krows], ss.at[i], sr.at[i], rad=sib))
                swaps[i].start()
                st[0, :, krows] = (whole[:, :CZ].T * dw).astype(BF16)

    for cp in stage_a:
        cp.wait()
    acc_a[...] = (part[pl.ds(cap * 32, 32)] + recv_a[1] + recv_a[2] + recv_a[3])
    recv_b[lat] = acc_a[pl.ds(lat * 2, 2)]
    stage_b = []
    for k in range(1, NLAT):
        to = lax.rem(lat + k, NLAT)
        cp = rcopy(acc_a.at[pl.ds(to * 2, 2)], recv_b.at[lat], pbs.at[k], pbr.at[k], lat=to)
        cp.start()
        stage_b.append(cp)

    def ship(res, first):
        outb[pl.ds(first, 2)] = res.T.astype(BF16).reshape(2, CY, CZ)

    def home(dest):
        return rcopy(outb.at[dest], rec.at[lat], rs.at[dest], rr.at[lat], lat=dest)

    def chunk(first):
        return pl.ds(pl.multiple_of(first * CY, 512), 512)

    near = pl.ds(pl.multiple_of(rad * HALF, HALF), HALF)
    far = pl.ds(pl.multiple_of(sib * HALF, HALF), HALF)
    first = lax.rem(mx + 2, 4) * 4
    res = jnp.dot(st[0, :, near], basis[near, chunk(first)], preferred_element_type=F32)
    for cp in swaps:
        cp.wait()
    res += jnp.dot(st[0, :, far], basis[far, chunk(first)], preferred_element_type=F32)
    ship(res, first)
    for q in range(2):
        home(first + q).start()

    @pl.loop(1, 6)
    def _(i):
        m = lax.rem(i, 3)
        first = lax.rem(mx + 2 + m * (3 * m - 5) // 2 + 4, 4) * 4 + (i // 3) * 2
        ship(jnp.dot(st[0], basis[:, chunk(first)], preferred_element_type=F32), first)
        for q in range(2):
            home(first + q).start()

    @pl.loop(0, 2)
    def _(i):
        first = mx * 4 + i * 2
        ship(jnp.dot(st[0], basis[:, chunk(first)], preferred_element_type=F32), first)
        for q in range(2):
            @pl.when(first + q != lat)
            def _():
                home(first + q).start()

    for cp in stage_b:
        cp.wait()
    acc_b[...] = jnp.sum(recv_b[...], axis=0)
    swap_c = rcopy(acc_b.at[sib], recv_c, pcs, pcr, rad=sib)
    swap_c.start()

    uv[lat] = flow[lat] + outb[lat].astype(F32)
    swap_c.wait()
    tect_ref[rad] = acc_b[rad]
    tect_ref[sib] = recv_c[...]
    pltpu.make_async_copy(arrived, arrived, g_send).wait()
    for dx, dz in steps:
        carry_out(dx, dz).wait_send()
    for src in range(NLAT):
        forward(src).wait_send()
    for dx, dz in ((2, 0), (2, 1), (1, 0), (1, 1), (3, 0), (3, 1), (2, 2), (2, 3), (1, 2), (1, 3), (3, 2), (3, 3),
                   (0, 1), (0, 3), (0, 2)):
        src = lax.rem(mx + 4 - dx, 4) * 4 + lax.rem(mz + dz, 4)
        rcopy(outb.at[src], rec.at[src], rs.at[src], rr.at[src], lat=src).wait_recv()
        uv[src] = flow[src] + rec[src].astype(F32)
    for dx, dz in steps:
        home(away(dx, dz)).wait_send()


def finish(flow, thermal, tect, flow_out, thermal_out, tect_out, sem):
    copies = [pltpu.make_async_copy(flow, flow_out, sem.at[0]), pltpu.make_async_copy(thermal, thermal_out, sem.at[1])]
    for cp in copies:
        cp.start()
    for r in range(2):
        for j in range(8):
            tect_out[0, r:r + 1, j * CZ:(j + 1) * CZ] = tect[r, j:j + 1, :]
    for cp in copies:
        cp.wait()


def body(forcing, viscosity, harmonic_basis, damping_weights, unit_plates):
    DMA = pltpu.SemaphoreType.DMA
    vm = pltpu.VMEM
    anys = pl.BlockSpec(memory_space=pl.ANY)
    vmem = pl.BlockSpec(memory_space=pltpu.VMEM)
    block = (CX, CY, CZ)
    tile = (CX, 8, CZ)
    face = (CY, CZ)
    flow, thermal, tect = pl.pallas_call(
        kernel,
        out_shape=(vm(block, F32), vm(block, F32), vm((2, 8, CZ), F32)),
        in_specs=[anys, anys, anys, vmem, vmem],
        out_specs=(vmem, vmem, vmem),
        scratch_shapes=[
            vm((18, CY, CZ), F32), vm((18, CY, CZ), F32), vm(block, BF16),
            vm((NY, NY), BF16), vm(block, BF16), vm(block, BF16), vm((HALF, 256), F32),
            vm((2, CZ, NY), BF16), vm(block, BF16), vm(block, BF16),
            vm(face, F32), vm(face, F32), vm(face, F32), vm(face, F32), vm(face, F32), vm(face, F32),
            vm(tile, F32), vm(tile, F32), vm(tile, F32), vm(tile, F32), vm(tile, F32),
            vm((CY // 2, CZ), F32), vm((CY // 2, CZ), F32),
            vm((128, 8, CZ), F32), vm((4, 32, 8, CZ), F32), vm((32, 8, CZ), F32),
            vm((NLAT, 2, 8, CZ), F32), vm((2, 8, CZ), F32), vm((8, CZ), F32),
            vm((1, CZ), F32), vm((128, 1, CZ), F32),
            DMA((2,)), DMA, pltpu.SemaphoreType.REGULAR, DMA((14,)), DMA((14,)), DMA, DMA,
            DMA((16,)), DMA((16,)), DMA((16,)), DMA((16,)), DMA((2,)), DMA((2,)), DMA((16,)), DMA((16,)),
            DMA((4,)), DMA((4,)), DMA((16,)), DMA((16,)), DMA, DMA,
        ],
        compiler_params=pltpu.CompilerParams(
            vmem_limit_bytes=56 << 20, collective_id=0, has_side_effects=True),
        name="adjoint",
    )(forcing, viscosity, harmonic_basis, damping_weights.reshape(1, NY), unit_plates.reshape(4, 128))
    return pl.pallas_call(
        finish,
        out_shape=(
            jax.ShapeDtypeStruct(block, F32),
            jax.ShapeDtypeStruct(block, F32),
            jax.ShapeDtypeStruct((1, 2, 8 * CZ), F32),
        ),
        in_specs=[vmem, vmem, vmem],
        out_specs=(anys, anys, vmem),
        scratch_shapes=[DMA((2,))],
        compiler_params=pltpu.CompilerParams(vmem_limit_bytes=16 << 20),
        name="finish",
    )(flow, thermal, tect)


def solution(mesh):
    in_specs = (
        P("cap", "lat", "rad"),
        P("cap", "lat", "rad"),
        P(),
        P(),
        P(("cap", "lat"), None, None),
    )
    out_specs = (
        P("cap", "lat", "rad"),
        P("cap", "lat", "rad"),
        P(("cap", "lat", "rad"), None, None),
    )
    return jax.shard_map(body, mesh=mesh, in_specs=in_specs, out_specs=out_specs, check_vma=False)
```

```python
import jax
import jax.numpy as jnp
from jax import lax
from jax.experimental import pallas as pl
from jax.experimental.pallas import tpu as pltpu
from jax.sharding import PartitionSpec as P

MESH = pl.DeviceIdType.MESH
F32 = jnp.float32
BF16 = jnp.bfloat16
CX, CY, CZ = 16, 256, 128
NY = 4096
RB = 64
NB = CY // RB
NLAT, NCAP, NRAD = 16, 4, 2
HALF = NY // 2


def iota(shape, dim):
    return lax.broadcasted_iota(jnp.int32, shape, dim)


def fold(x):
    return jnp.sum(x.reshape(x.shape[0] // 8, 8, CZ), axis=0)


def kernel(b_hbm, v_hbm, basis_hbm, damp_ref, plates_ref, flow, uv, tect_ref,
           bp, vp, vy, vz, fb, basis, xm, xo, coef, st, outb, rec,
           pb, pv, pu, qb, qv, qu, ybm, ybp, yvm, yvp, yu, xup, xdn,
           part, recv_a, acc_a, recv_b, acc_b, recv_c, mine, rows,
           loc_sem, basis_sem, deep, hs, hr, g_send, g_recv,
           as_, ar_, fs, fr, ss, sr, rs, rr, pas, par, pbs, pbr, pcs, pcr):
    cap = lax.axis_index("cap")
    lat = lax.axis_index("lat")
    rad = lax.axis_index("rad")
    mx = lat // 4
    mz = lax.rem(lat, 4)
    up_cap, dn_cap = lax.rem(cap + 1, NCAP), lax.rem(cap + NCAP - 1, NCAP)
    up_lat, dn_lat = lax.rem(lat + 1, NLAT), lax.rem(lat + NLAT - 1, NLAT)
    sib = 1 - rad

    loads = [
        pltpu.make_async_copy(b_hbm, bp.at[1:17], loc_sem.at[0]),
        pltpu.make_async_copy(v_hbm, vp.at[1:17], loc_sem.at[1]),
    ]
    for cp in loads:
        cp.start()

    bar = pltpu.get_barrier_semaphore()
    column = [(k // 2, k % 2) for k in range(1, 8)]

    def tell(sem, **dev):
        pl.semaphore_signal(sem, inc=1, device_id=dev, device_id_type=MESH)

    def fellow(k):
        return {"cap": lax.rem(cap + k[0], NCAP), "rad": lax.rem(rad + k[1], NRAD)}

    for k in column:
        tell(bar, **fellow(k))
    for k in range(1, NLAT):
        tell(bar, lat=lax.rem(lat + k, NLAT))
    pl.semaphore_wait(bar, 22)

    def rcopy(src, dst, ssem, rsem, **dev):
        return pltpu.make_async_remote_copy(
            src_ref=src, dst_ref=dst, send_sem=ssem, recv_sem=rsem, device_id=dev, device_id_type=MESH)

    yh, xh = [], []
    for q, (hbm, pad, lo, hi) in enumerate(((b_hbm, bp, ybm, ybp), (v_hbm, vp, yvm, yvp))):
        yh.append(rcopy(hbm.at[:, 248:256, :], lo, hs.at[q], hr.at[q], lat=up_lat))
        yh.append(rcopy(hbm.at[:, 0:8, :], hi, hs.at[2 + q], hr.at[2 + q], lat=dn_lat))
        xh.append(rcopy(hbm.at[15], pad.at[0], hs.at[4 + q], hr.at[4 + q], cap=up_cap))
        xh.append(rcopy(hbm.at[0], pad.at[17], hs.at[6 + q], hr.at[6 + q], cap=dn_cap))
    for cp in xh + yh:
        cp.start()
    for cp in loads:
        cp.wait()
    lane = iota((RB, CZ), 1)
    row = iota((RB, CZ), 0)
    edge = (lane == 0) | (lane == CZ - 1)

    def pack(ref, base, dst):
        for yb in range(NB):
            rows_ = slice(yb * RB, (yb + 1) * RB)
            acc = jnp.zeros((RB, CZ), F32)
            for x in range(CX):
                acc = jnp.where(lane // 2 == x, pltpu.roll(ref[base + x, rows_, :], 2 * x + 1, 1), acc)
            dst[rows_, :] = acc

    wide = iota((CY, CZ), 1)
    facing = lax.rem(wide, 2) == rad

    def across(q):
        turned = jnp.where(rad == 0, pltpu.roll(q, CZ - 1, 1), pltpu.roll(q, 1, 1))
        return jnp.where(facing, turned, 0.0)

    pack(bp, 1, pb)
    zb = rcopy(pb, qb, hs.at[8], hr.at[8], rad=sib)
    zb.start()
    pack(vp, 1, pv)
    zv = rcopy(pv, qv, hs.at[9], hr.at[9], rad=sib)
    zv.start()
    for k in column:
        tell(deep, **fellow(k))
    basis_cp = pltpu.make_async_copy(basis_hbm, basis, basis_sem)
    basis_cp.start()
    zero = jnp.zeros((8, CZ), F32)

    def square(x, s):
        b0 = bp[x]
        return s + jnp.sum((b0 * b0).reshape(4, 8, 8, CZ), axis=1)

    m0 = jnp.sum(lax.fori_loop(1, 17, square, jnp.zeros((4, 8, CZ), F32)), axis=0)
    zb.wait()
    zv.wait()
    qv[...] = pv[...] + across(qv[...])
    qb[...] = qv[...] * (pb[...] - across(qb[...]))

    def plane(X, carry):
        shift = CZ + 1 - 2 * X
        before = jnp.zeros((1, CZ), F32)
        for yb in range(NB):
            y0 = yb * RB
            rows_ = slice(y0, y0 + RB)
            b0, v0 = bp[X, rows_, :], vp[X, rows_, :]
            acc = (v0 + vp[X + 1, rows_, :]) * (b0 - bp[X + 1, rows_, :])
            acc += (v0 + vp[X - 1, rows_, :]) * (b0 - bp[X - 1, rows_, :])
            if yb < NB - 1:
                near = slice(y0 + 1, y0 + 1 + RB)
                pair = v0 + vp[X, near, :]
                flux = pair * (b0 - bp[X, near, :])
            else:
                pair = jnp.where(row < RB - 1, v0 + pltpu.roll(v0, RB - 1, 0), 0.0)
                flux = pair * (b0 - pltpu.roll(b0, RB - 1, 0))
            vy[X - 1, rows_, :] = pair
            acc += flux - jnp.where(row > 0, pltpu.roll(flux, 1, 0), before)
            before = flux[RB - 1:RB, :]
            pair = jnp.where(lane < CZ - 1, v0 + pltpu.roll(v0, CZ - 1, 1), 0.0)
            vz[X - 1, rows_, :] = pair
            flux = pair * (b0 - pltpu.roll(b0, CZ - 1, 1))
            acc += flux - pltpu.roll(flux, 1, 1)
            acc += jnp.where(edge, pltpu.roll(qb[rows_, :], shift, 1), 0.0)
            uv[X - 1, rows_, :] = acc
        return carry

    low_y = jnp.where(lat == 0, 0.0, 1.0).astype(F32)
    high_y = jnp.where(lat == NLAT - 1, 0.0, 1.0).astype(F32)

    def lat_faces(a, b):
        for at, bh, vh, far, keep in ((0, ybm, yvm, 7, low_y), (255, ybp, yvp, 0, high_y)):
            here = slice(at, at + 1)
            there = slice(far, far + 1)
            uv[a:b, here, :] += ((vp[a + 1:b + 1, here, :] + keep * vh[a:b, there, :])
                                 * (bp[a + 1:b + 1, here, :] - keep * bh[a:b, there, :]))

    def energy(x, sums, with_x):
        n1, n2, n3 = sums
        for yb in range(NB):
            y0 = yb * RB
            rows_ = slice(y0, y0 + RB)
            u0, b0 = uv[x, rows_, :], bp[x + 1, rows_, :]
            d = u0 - pltpu.roll(u0, CZ - 1, 1)
            acc = vz[x, rows_, :] * (d * d)
            if with_x:
                d = u0 - uv[x + 1, rows_, :]
                acc += (vp[x + 1, rows_, :] + vp[x + 2, rows_, :]) * (d * d)
            if yb < NB - 1:
                d = u0 - uv[x, y0 + 1:y0 + 1 + RB, :]
            else:
                d = u0 - pltpu.roll(u0, RB - 1, 0)
            acc += vy[x, rows_, :] * (d * d)
            n1 += fold(b0 * u0)
            n2 += fold(u0 * u0)
            n3 += fold(acc)
        return n1, n2, n3

    lax.fori_loop(2, 16, plane, 0)
    for cp in yh:
        cp.wait()
    lat_faces(1, 15)
    for cp in xh:
        cp.wait()
    for side, at in ((0, 0), (NCAP - 1, 17)):
        @pl.when(cap == side)
        def _():
            bp[at] = jnp.zeros((CY, CZ), F32)
            vp[at] = jnp.zeros((CY, CZ), F32)
    plane(1, 0)
    plane(16, 0)
    lat_faces(0, 1)
    lat_faces(15, 16)

    mid = CY // 2
    ux = [
        rcopy(uv.at[0, 0:mid], xup, hs.at[10], hr.at[10], cap=dn_cap),
        rcopy(uv.at[15, mid:CY], xdn, hs.at[11], hr.at[11], cap=up_cap),
    ]
    for cp in ux:
        cp.start()
    uy = rcopy(uv.at[:, 0:8, :], yu, hs.at[12], hr.at[12], lat=dn_lat)
    uy.start()
    pack(uv, 0, pu)
    uz = rcopy(pu, qu, hs.at[13], hr.at[13], rad=sib)
    uz.start()
    sums = lax.fori_loop(0, 15, lambda x, s: energy(x, s, True), (zero, zero, zero))
    n1, n2, n3 = energy(15, sums, False)
    u0, u15 = uv[0, 0:mid], uv[15, mid:CY]
    first = jnp.where(cap == 0, 1.0, 0.0).astype(F32)
    last = jnp.where(cap == NCAP - 1, 1.0, 0.0).astype(F32)
    n3 += fold(first * vp[1, 0:mid] * (u0 * u0)) + fold(last * vp[16, mid:CY] * (u15 * u15))
    u0 = uv[:, 0:1, :]
    edge_row = jnp.sum((1.0 - low_y) * vp[1:17, 0:1, :] * (u0 * u0), axis=0)
    uz.wait()
    d = pu[...] - across(qu[...])
    n3 += fold(jnp.where(facing, 0.5, 1.0) * qv[...] * (d * d))
    uy.wait()
    d = uv[:, 255:256, :] - high_y * yu[:, 0:1, :]
    edge_row += jnp.sum((vp[1:17, 255:256, :] + high_y * yvp[:, 0:1, :]) * (d * d), axis=0)
    for cp in ux:
        cp.wait()
    d = uv[15, 0:mid] - (1.0 - last) * xup[...]
    n3 += fold((vp[16, 0:mid] + vp[17, 0:mid]) * (d * d))
    d = uv[0, mid:CY] - (1.0 - first) * xdn[...]
    n3 += fold((vp[1, mid:CY] + vp[0, mid:CY]) * (d * d))

    lane1 = iota((1, CZ), 1)
    line = jnp.zeros((1, CZ), F32)
    for q, s in enumerate((m0, n1, n2, n3)):
        s = jnp.sum(s, axis=0, keepdims=True)
        if q == 3:
            s = s + edge_row
        line = jnp.where(lane1 == q, jnp.sum(s, axis=1, keepdims=True), line)
    mine[...] = line
    place = (cap * NLAT + lat) * NRAD + rad
    rows[place] = line
    pl.semaphore_wait(deep, 7)
    ring = (0, 1, 2, 1)
    others = sorted(((c, x, z, r) for c in range(4) for x in range(4) for z in range(4) for r in range(2)),
                    key=lambda o: -(ring[o[0]] + ring[o[1]] + ring[o[2]]))
    for c, x, z, r in others:
        if (c, x, z, r) != (0, 0, 0, 0):
            rcopy(mine, rows.at[place], g_send, g_recv,
                  cap=lax.rem(cap + c, NCAP), lat=lax.rem(mx + x, 4) * 4 + lax.rem(mz + z, 4),
                  rad=lax.rem(rad + r, NRAD)).start()
    arrived = rows.at[pl.ds(0, 127)]
    pltpu.make_async_copy(arrived, arrived, g_recv).wait()
    tot = jnp.sum(rows[...], axis=0)
    t0, e1, e2, e3 = [jnp.sum(jnp.where(lane1 == q, tot, 0.0), axis=1, keepdims=True) for q in range(4)]
    e1, e2, e3 = 0.5 * e1 / t0, 0.25 * e2 / t0, 0.125 * e3 / t0
    step0 = 1.0 / (1.0 + e1)
    ratio = jnp.maximum((e2 - e1 * e1) * step0 * step0, 0.0)
    g, h = (1.0 - step0) + ratio, -step0
    pap = g * g * (1.0 + e1) + 2.0 * g * h * (e1 + e2) + h * h * (e2 + e3)
    step1 = ratio / jnp.maximum(jnp.maximum(pap, ratio), 1e-30)
    alpha, beta = step0 + step1 * g, 0.5 * step1 * h

    def away(dx, dz):
        return lax.rem(mx + dx, 4) * 4 + lax.rem(mz + dz, 4)

    def solve(x):
        f = alpha * bp[x + 1] + beta * uv[x]
        flow[x] = f
        fb[x] = f.astype(BF16)

    steps = [(1, 2), (3, 2), (1, 1), (3, 1), (1, 3), (3, 3), (1, 0), (3, 0), (2, 2), (0, 1), (2, 1), (0, 3), (2, 3), (0, 2), (2, 0)]

    def carry_out(dx, dz):
        dest = away(dx, dz)
        k = dx * 4 + dz
        return rcopy(fb.at[dest], xm.at[lat], as_.at[k], ar_.at[k], lat=dest)

    for dx, dz in steps:
        solve(away(dx, dz))
        carry_out(dx, dz).start()
    solve(lat)
    xm[lat] = fb[lat]

    def forward(src):
        return rcopy(xm.at[src], xo.at[src], fs.at[src], fr.at[src], rad=sib)

    forward(lat).start()

    @pl.loop(0, CX)
    def _(x):
        uv[x] = vp[x + 1] * flow[x]
    plate_row = iota((128, 128), 0)
    hots = [jnp.where(plates_ref[q:q + 1, :] == plate_row, 1.0, 0.0).astype(BF16) for q in range(4)]
    hot = jnp.concatenate(hots, axis=1)
    flat = uv.reshape(CX * CY, CZ)
    pflat = part.reshape(128 * 8, CZ)
    for j in range(8):
        u = flat[pl.ds(j, 512, stride=8), :]
        hi = u.astype(BF16)
        lo = (u - hi.astype(F32)).astype(BF16)
        pflat[pl.ds(j, 128, stride=8), :] = (
            jnp.dot(hot, hi, preferred_element_type=F32) + jnp.dot(hot, lo, preferred_element_type=F32))
    stage_a = []
    for k in range(1, NCAP):
        to = lax.rem(cap + k, NCAP)
        cp = rcopy(part.at[pl.ds(to * 32, 32)], recv_a.at[k], pas.at[k], par.at[k], cap=to)
        cp.start()
        stage_a.append(cp)

    basis_cp.wait()
    krow = rad * HALF
    swaps = []
    order = (1, 3, 0, 2)

    def block_of(g4):
        return lax.rem(mx + 4 - g4, 4)

    stage_b = []
    for step in range(5):
        if step == 2:
            for cp in stage_a:
                cp.wait()
            acc_a[...] = (part[pl.ds(cap * 32, 32)] + recv_a[1] + recv_a[2] + recv_a[3])
            recv_b[lat] = acc_a[pl.ds(lat * 2, 2)]
            for k in range(1, NLAT):
                to = lax.rem(lat + k, NLAT)
                cp = rcopy(acc_a.at[pl.ds(to * 2, 2)], recv_b.at[lat], pbs.at[k], pbr.at[k], lat=to)
                cp.start()
                stage_b.append(cp)
        if step < 4:
            g4 = order[step]
            for dz in (2, 1, 3, 0):
                if g4 or dz:
                    src = block_of(g4) * 4 + lax.rem(mz + 4 - dz, 4)
                    k = g4 * 4 + dz
                    rcopy(fb.at[src], xm.at[src], as_.at[k], ar_.at[k], lat=src).wait_recv()
                    forward(src).start()
        if step == 0:
            continue
        gx = block_of(order[step - 1])
        for q in range(4):
            forward(gx * 4 + q).wait_recv()
        cols = pl.ds(pl.multiple_of(gx * 1024, 1024), 1024)
        xs = jnp.concatenate(
            [xm[pl.ds(gx * 4, 4)].reshape(1024, CZ), xo[pl.ds(gx * 4, 4)].reshape(1024, CZ)], axis=1)
        for i in range(2):
            krows = pl.ds(pl.multiple_of(krow + i * 1024, 1024), 1024)
            crow = slice(i * 1024, (i + 1) * 1024)
            prod = jnp.dot(basis[krows, cols], xs, preferred_element_type=F32)
            if step == 1:
                coef[crow, :] = prod
            elif step < 4:
                coef[crow, :] += prod
            else:
                whole = coef[crow, :] + prod
                dw = damp_ref[:, krows]
                st[1, :, krows] = (whole[:, CZ:].T * dw).astype(BF16)
                swaps.append(rcopy(st.at[1, :, krows], st.at[0, :, krows], ss.at[i], sr.at[i], rad=sib))
                swaps[i].start()
                st[0, :, krows] = (whole[:, :CZ].T * dw).astype(BF16)

    for cp in stage_b:
        cp.wait()
    acc_b[...] = jnp.sum(recv_b[...], axis=0)
    swap_c = rcopy(acc_b.at[sib], recv_c, pcs, pcr, rad=sib)
    swap_c.start()

    def ship(res, first):
        outb[pl.ds(first, 2)] = res.T.astype(BF16).reshape(2, CY, CZ)

    def home(dest):
        return rcopy(outb.at[dest], rec.at[lat], rs.at[dest], rr.at[lat], lat=dest)

    def chunk(first):
        return pl.ds(pl.multiple_of(first * CY, 512), 512)

    near = pl.ds(pl.multiple_of(rad * HALF, HALF), HALF)
    far = pl.ds(pl.multiple_of(sib * HALF, HALF), HALF)
    first = lax.rem(mx + 1, 4) * 4
    res = jnp.dot(st[0, :, near], basis[near, chunk(first)], preferred_element_type=F32)
    for cp in swaps:
        cp.wait()
    res += jnp.dot(st[0, :, far], basis[far, chunk(first)], preferred_element_type=F32)
    ship(res, first)
    for q in range(2):
        home(first + q).start()

    @pl.loop(1, 4)
    def _(i):
        first = lax.rem(mx + 1 + 2 * lax.rem(i, 2), 4) * 4 + (i // 2) * 2
        ship(jnp.dot(st[0], basis[:, chunk(first)], preferred_element_type=F32), first)
        for q in range(2):
            home(first + q).start()

    @pl.loop(0, 4)
    def _(i):
        first = lax.rem(mx + 2 - 2 * lax.rem(i, 2), 4) * 4 + (i // 2) * 2
        ship(jnp.dot(st[0], basis[:, chunk(first)], preferred_element_type=F32), first)
        for q in range(2):
            @pl.when(first + q != lat)
            def _():
                home(first + q).start()

    uv[lat] = flow[lat] + outb[lat].astype(F32)
    swap_c.wait()
    tect_ref[rad] = acc_b[rad]
    tect_ref[sib] = recv_c[...]
    pltpu.make_async_copy(arrived, arrived, g_send).wait()
    for dx, dz in steps:
        carry_out(dx, dz).wait_send()
    for src in range(NLAT):
        forward(src).wait_send()
    for dx, dz in ((1, 0), (1, 1), (3, 0), (3, 1), (1, 2), (1, 3), (3, 2), (3, 3), (2, 0), (2, 1), (0, 1), (2, 2), (2, 3),
                   (0, 3), (0, 2)):
        src = lax.rem(mx + 4 - dx, 4) * 4 + lax.rem(mz + dz, 4)
        rcopy(outb.at[src], rec.at[src], rs.at[src], rr.at[src], lat=src).wait_recv()
        uv[src] = flow[src] + rec[src].astype(F32)
    for dx, dz in steps:
        home(away(dx, dz)).wait_send()


def finish(flow, thermal, tect, flow_out, thermal_out, tect_out, sem):
    copies = [pltpu.make_async_copy(flow, flow_out, sem.at[0]), pltpu.make_async_copy(thermal, thermal_out, sem.at[1])]
    for cp in copies:
        cp.start()
    for r in range(2):
        for j in range(8):
            tect_out[0, r:r + 1, j * CZ:(j + 1) * CZ] = tect[r, j:j + 1, :]
    for cp in copies:
        cp.wait()


def body(forcing, viscosity, harmonic_basis, damping_weights, unit_plates):
    DMA = pltpu.SemaphoreType.DMA
    vm = pltpu.VMEM
    anys = pl.BlockSpec(memory_space=pl.ANY)
    vmem = pl.BlockSpec(memory_space=pltpu.VMEM)
    block = (CX, CY, CZ)
    tile = (CX, 8, CZ)
    face = (CY, CZ)
    flow, thermal, tect = pl.pallas_call(
        kernel,
        out_shape=(vm(block, F32), vm(block, F32), vm((2, 8, CZ), F32)),
        in_specs=[anys, anys, anys, vmem, vmem],
        out_specs=(vmem, vmem, vmem),
        scratch_shapes=[
            vm((18, CY, CZ), F32), vm((18, CY, CZ), F32), vm(block, F32), vm(block, F32), vm(block, BF16),
            vm((NY, NY), BF16), vm(block, BF16), vm(block, BF16), vm((HALF, 256), F32),
            vm((2, CZ, NY), BF16), vm(block, BF16), vm(block, BF16),
            vm(face, F32), vm(face, F32), vm(face, F32), vm(face, F32), vm(face, F32), vm(face, F32),
            vm(tile, F32), vm(tile, F32), vm(tile, F32), vm(tile, F32), vm(tile, F32),
            vm((CY // 2, CZ), F32), vm((CY // 2, CZ), F32),
            vm((128, 8, CZ), F32), vm((4, 32, 8, CZ), F32), vm((32, 8, CZ), F32),
            vm((NLAT, 2, 8, CZ), F32), vm((2, 8, CZ), F32), vm((8, CZ), F32),
            vm((1, CZ), F32), vm((128, 1, CZ), F32),
            DMA((2,)), DMA, pltpu.SemaphoreType.REGULAR, DMA((14,)), DMA((14,)), DMA, DMA,
            DMA((16,)), DMA((16,)), DMA((16,)), DMA((16,)), DMA((2,)), DMA((2,)), DMA((16,)), DMA((16,)),
            DMA((4,)), DMA((4,)), DMA((16,)), DMA((16,)), DMA, DMA,
        ],
        compiler_params=pltpu.CompilerParams(
            vmem_limit_bytes=56 << 20, collective_id=0, has_side_effects=True),
        name="adjoint",
    )(forcing, viscosity, harmonic_basis, damping_weights.reshape(1, NY), unit_plates.reshape(4, 128))
    return pl.pallas_call(
        finish,
        out_shape=(
            jax.ShapeDtypeStruct(block, F32),
            jax.ShapeDtypeStruct(block, F32),
            jax.ShapeDtypeStruct((1, 2, 8 * CZ), F32),
        ),
        in_specs=[vmem, vmem, vmem],
        out_specs=(anys, anys, vmem),
        scratch_shapes=[DMA((2,))],
        compiler_params=pltpu.CompilerParams(vmem_limit_bytes=16 << 20),
        name="finish",
    )(flow, thermal, tect)


def solution(mesh):
    in_specs = (
        P("cap", "lat", "rad"),
        P("cap", "lat", "rad"),
        P(),
        P(),
        P(("cap", "lat"), None, None),
    )
    out_specs = (
        P("cap", "lat", "rad"),
        P("cap", "lat", "rad"),
        P(("cap", "lat", "rad"), None, None),
    )
    return jax.shard_map(body, mesh=mesh, in_specs=in_specs, out_specs=out_specs, check_vma=False)
```

```python
import jax
import jax.numpy as jnp
from jax import lax
from jax.experimental import pallas as pl
from jax.experimental.pallas import tpu as pltpu
from jax.sharding import PartitionSpec as P

MESH = pl.DeviceIdType.MESH
F32 = jnp.float32
BF16 = jnp.bfloat16
CX, CY, CZ = 16, 256, 128
NY = 4096
RB = 64
NB = CY // RB
NLAT, NCAP, NRAD = 16, 4, 2
HALF = NY // 2


def iota(shape, dim):
    return lax.broadcasted_iota(jnp.int32, shape, dim)


def fold(x):
    return jnp.sum(x.reshape(x.shape[0] // 8, 8, CZ), axis=0)


def kernel(b_hbm, v_hbm, basis_hbm, damp_ref, plates_ref, flow, uv, tect_ref,
           bp, vp, vy, vz, fb, basis, xm, xo, coef, dampc, st, outb, rec,
           pb, pv, pu, qb, qv, qu, ybm, ybp, yvm, yvp, yu, xup, xdn,
           part, recv_a, acc_a, recv_b, acc_b, recv_c, mine, rows,
           loc_sem, basis_sem, deep, hs, hr, g_send, g_recv,
           as_, ar_, fs, fr, ss, sr, rs, rr, pas, par, pbs, pbr, pcs, pcr):
    cap = lax.axis_index("cap")
    lat = lax.axis_index("lat")
    rad = lax.axis_index("rad")
    mx = lat // 4
    mz = lax.rem(lat, 4)
    up_cap, dn_cap = lax.rem(cap + 1, NCAP), lax.rem(cap + NCAP - 1, NCAP)
    up_lat, dn_lat = lax.rem(lat + 1, NLAT), lax.rem(lat + NLAT - 1, NLAT)
    sib = 1 - rad

    loads = [
        pltpu.make_async_copy(b_hbm, bp.at[1:17], loc_sem.at[0]),
        pltpu.make_async_copy(v_hbm, vp.at[1:17], loc_sem.at[1]),
    ]
    for cp in loads:
        cp.start()

    bar = pltpu.get_barrier_semaphore()
    column = [(k // 2, k % 2) for k in range(1, 8)]

    def tell(sem, **dev):
        pl.semaphore_signal(sem, inc=1, device_id=dev, device_id_type=MESH)

    def fellow(k):
        return {"cap": lax.rem(cap + k[0], NCAP), "rad": lax.rem(rad + k[1], NRAD)}

    for k in column:
        tell(bar, **fellow(k))
    for k in range(1, NLAT):
        tell(bar, lat=lax.rem(lat + k, NLAT))
    pl.semaphore_wait(bar, 22)

    def rcopy(src, dst, ssem, rsem, **dev):
        return pltpu.make_async_remote_copy(
            src_ref=src, dst_ref=dst, send_sem=ssem, recv_sem=rsem, device_id=dev, device_id_type=MESH)

    yh, xh = [], []
    for q, (hbm, pad, lo, hi) in enumerate(((b_hbm, bp, ybm, ybp), (v_hbm, vp, yvm, yvp))):
        yh.append(rcopy(hbm.at[:, 248:256, :], lo, hs.at[q], hr.at[q], lat=up_lat))
        yh.append(rcopy(hbm.at[:, 0:8, :], hi, hs.at[2 + q], hr.at[2 + q], lat=dn_lat))
        xh.append(rcopy(hbm.at[15], pad.at[0], hs.at[4 + q], hr.at[4 + q], cap=up_cap))
        xh.append(rcopy(hbm.at[0], pad.at[17], hs.at[6 + q], hr.at[6 + q], cap=dn_cap))
    for cp in xh + yh:
        cp.start()
    for cp in loads:
        cp.wait()
    lane = iota((RB, CZ), 1)
    row = iota((RB, CZ), 0)
    edge = (lane == 0) | (lane == CZ - 1)

    def pack(ref, base, dst):
        for yb in range(NB):
            rows_ = slice(yb * RB, (yb + 1) * RB)
            acc = jnp.zeros((RB, CZ), F32)
            for x in range(CX):
                acc = jnp.where(lane // 2 == x, pltpu.roll(ref[base + x, rows_, :], 2 * x + 1, 1), acc)
            dst[rows_, :] = acc

    wide = iota((CY, CZ), 1)
    facing = lax.rem(wide, 2) == rad

    def across(q):
        turned = jnp.where(rad == 0, pltpu.roll(q, CZ - 1, 1), pltpu.roll(q, 1, 1))
        return jnp.where(facing, turned, 0.0)

    pack(bp, 1, pb)
    zb = rcopy(pb, qb, hs.at[8], hr.at[8], rad=sib)
    zb.start()
    pack(vp, 1, pv)
    zv = rcopy(pv, qv, hs.at[9], hr.at[9], rad=sib)
    zv.start()
    for k in column:
        tell(deep, **fellow(k))
    basis_cp = pltpu.make_async_copy(basis_hbm, basis, basis_sem)
    basis_cp.start()
    zero = jnp.zeros((8, CZ), F32)

    def square(x, s):
        b0 = bp[x]
        return s + jnp.sum((b0 * b0).reshape(4, 8, 8, CZ), axis=1)

    m0 = jnp.sum(lax.fori_loop(1, 17, square, jnp.zeros((4, 8, CZ), F32)), axis=0)
    zb.wait()
    zv.wait()
    qv[...] = pv[...] + across(qv[...])
    qb[...] = qv[...] * (pb[...] - across(qb[...]))

    def plane(X, carry):
        shift = CZ + 1 - 2 * X
        before = jnp.zeros((1, CZ), F32)
        for yb in range(NB):
            y0 = yb * RB
            rows_ = slice(y0, y0 + RB)
            b0, v0 = bp[X, rows_, :], vp[X, rows_, :]
            acc = (v0 + vp[X + 1, rows_, :]) * (b0 - bp[X + 1, rows_, :])
            acc += (v0 + vp[X - 1, rows_, :]) * (b0 - bp[X - 1, rows_, :])
            if yb < NB - 1:
                near = slice(y0 + 1, y0 + 1 + RB)
                pair = v0 + vp[X, near, :]
                flux = pair * (b0 - bp[X, near, :])
            else:
                pair = jnp.where(row < RB - 1, v0 + pltpu.roll(v0, RB - 1, 0), 0.0)
                flux = pair * (b0 - pltpu.roll(b0, RB - 1, 0))
            vy[X - 1, rows_, :] = pair
            acc += flux - jnp.where(row > 0, pltpu.roll(flux, 1, 0), before)
            before = flux[RB - 1:RB, :]
            pair = jnp.where(lane < CZ - 1, v0 + pltpu.roll(v0, CZ - 1, 1), 0.0)
            vz[X - 1, rows_, :] = pair
            flux = pair * (b0 - pltpu.roll(b0, CZ - 1, 1))
            acc += flux - pltpu.roll(flux, 1, 1)
            acc += jnp.where(edge, pltpu.roll(qb[rows_, :], shift, 1), 0.0)
            uv[X - 1, rows_, :] = acc
        return carry

    low_y = jnp.where(lat == 0, 0.0, 1.0).astype(F32)
    high_y = jnp.where(lat == NLAT - 1, 0.0, 1.0).astype(F32)

    def lat_faces(a, b):
        for at, bh, vh, far, keep in ((0, ybm, yvm, 7, low_y), (255, ybp, yvp, 0, high_y)):
            here = slice(at, at + 1)
            there = slice(far, far + 1)
            uv[a:b, here, :] += ((vp[a + 1:b + 1, here, :] + keep * vh[a:b, there, :])
                                 * (bp[a + 1:b + 1, here, :] - keep * bh[a:b, there, :]))

    def energy(x, sums, with_x):
        n1, n2, n3 = sums
        for yb in range(NB):
            y0 = yb * RB
            rows_ = slice(y0, y0 + RB)
            u0, b0 = uv[x, rows_, :], bp[x + 1, rows_, :]
            d = u0 - pltpu.roll(u0, CZ - 1, 1)
            acc = vz[x, rows_, :] * (d * d)
            if with_x:
                d = u0 - uv[x + 1, rows_, :]
                acc += (vp[x + 1, rows_, :] + vp[x + 2, rows_, :]) * (d * d)
            if yb < NB - 1:
                d = u0 - uv[x, y0 + 1:y0 + 1 + RB, :]
            else:
                d = u0 - pltpu.roll(u0, RB - 1, 0)
            acc += vy[x, rows_, :] * (d * d)
            n1 += fold(b0 * u0)
            n2 += fold(u0 * u0)
            n3 += fold(acc)
        return n1, n2, n3

    lax.fori_loop(2, 16, plane, 0)
    for cp in yh:
        cp.wait()
    lat_faces(1, 15)
    for cp in xh:
        cp.wait()
    for side, at in ((0, 0), (NCAP - 1, 17)):
        @pl.when(cap == side)
        def _():
            bp[at] = jnp.zeros((CY, CZ), F32)
            vp[at] = jnp.zeros((CY, CZ), F32)
    plane(1, 0)
    plane(16, 0)
    lat_faces(0, 1)
    lat_faces(15, 16)

    mid = CY // 2
    ux = [
        rcopy(uv.at[0, 0:mid], xup, hs.at[10], hr.at[10], cap=dn_cap),
        rcopy(uv.at[15, mid:CY], xdn, hs.at[11], hr.at[11], cap=up_cap),
    ]
    for cp in ux:
        cp.start()
    uy = rcopy(uv.at[:, 0:8, :], yu, hs.at[12], hr.at[12], lat=dn_lat)
    uy.start()
    pack(uv, 0, pu)
    uz = rcopy(pu, qu, hs.at[13], hr.at[13], rad=sib)
    uz.start()
    sums = lax.fori_loop(0, 15, lambda x, s: energy(x, s, True), (zero, zero, zero))
    n1, n2, n3 = energy(15, sums, False)
    u0, u15 = uv[0, 0:mid], uv[15, mid:CY]
    first = jnp.where(cap == 0, 1.0, 0.0).astype(F32)
    last = jnp.where(cap == NCAP - 1, 1.0, 0.0).astype(F32)
    n3 += fold(first * vp[1, 0:mid] * (u0 * u0)) + fold(last * vp[16, mid:CY] * (u15 * u15))
    u0 = uv[:, 0:1, :]
    edge_row = jnp.sum((1.0 - low_y) * vp[1:17, 0:1, :] * (u0 * u0), axis=0)
    uz.wait()
    d = pu[...] - across(qu[...])
    n3 += fold(jnp.where(facing, 0.5, 1.0) * qv[...] * (d * d))
    uy.wait()
    d = uv[:, 255:256, :] - high_y * yu[:, 0:1, :]
    edge_row += jnp.sum((vp[1:17, 255:256, :] + high_y * yvp[:, 0:1, :]) * (d * d), axis=0)
    for cp in ux:
        cp.wait()
    d = uv[15, 0:mid] - (1.0 - last) * xup[...]
    n3 += fold((vp[16, 0:mid] + vp[17, 0:mid]) * (d * d))
    d = uv[0, mid:CY] - (1.0 - first) * xdn[...]
    n3 += fold((vp[1, mid:CY] + vp[0, mid:CY]) * (d * d))

    lane1 = iota((1, CZ), 1)
    line = jnp.zeros((1, CZ), F32)
    for q, s in enumerate((m0, n1, n2, n3)):
        s = jnp.sum(s, axis=0, keepdims=True)
        if q == 3:
            s = s + edge_row
        line = jnp.where(lane1 == q, jnp.sum(s, axis=1, keepdims=True), line)
    mine[...] = line
    place = (cap * NLAT + lat) * NRAD + rad
    rows[place] = line
    pl.semaphore_wait(deep, 7)
    ring = (0, 1, 2, 1)
    others = sorted(((c, x, z, r) for c in range(4) for x in range(4) for z in range(4) for r in range(2)),
                    key=lambda o: -(ring[o[0]] + ring[o[1]] + ring[o[2]]))
    for c, x, z, r in others:
        if (c, x, z, r) != (0, 0, 0, 0):
            rcopy(mine, rows.at[place], g_send, g_recv,
                  cap=lax.rem(cap + c, NCAP), lat=lax.rem(mx + x, 4) * 4 + lax.rem(mz + z, 4),
                  rad=lax.rem(rad + r, NRAD)).start()
    arrived = rows.at[pl.ds(0, 127)]
    pltpu.make_async_copy(arrived, arrived, g_recv).wait()
    tot = jnp.sum(rows[...], axis=0)
    t0, e1, e2, e3 = [jnp.sum(jnp.where(lane1 == q, tot, 0.0), axis=1, keepdims=True) for q in range(4)]
    e1, e2, e3 = 0.5 * e1 / t0, 0.25 * e2 / t0, 0.125 * e3 / t0
    step0 = 1.0 / (1.0 + e1)
    ratio = jnp.maximum((e2 - e1 * e1) * step0 * step0, 0.0)
    g, h = (1.0 - step0) + ratio, -step0
    pap = g * g * (1.0 + e1) + 2.0 * g * h * (e1 + e2) + h * h * (e2 + e3)
    step1 = ratio / jnp.maximum(jnp.maximum(pap, ratio), 1e-30)
    alpha, beta = step0 + step1 * g, 0.5 * step1 * h

    def away(dx, dz):
        return lax.rem(mx + dx, 4) * 4 + lax.rem(mz + dz, 4)

    def solve(x):
        f = alpha * bp[x + 1] + beta * uv[x]
        flow[x] = f
        fb[x] = f.astype(BF16)

    steps = [(1, 2), (3, 2), (1, 1), (3, 1), (1, 3), (3, 3), (1, 0), (3, 0), (2, 2), (0, 1), (2, 1), (0, 3), (2, 3), (0, 2), (2, 0)]

    def carry_out(dx, dz):
        dest = away(dx, dz)
        k = dx * 4 + dz
        return rcopy(fb.at[dest], xm.at[lat], as_.at[k], ar_.at[k], lat=dest)

    for dx, dz in steps:
        solve(away(dx, dz))
        carry_out(dx, dz).start()
    solve(lat)
    xm[lat] = fb[lat]

    def forward(src):
        return rcopy(xm.at[src], xo.at[src], fs.at[src], fr.at[src], rad=sib)

    forward(lat).start()

    @pl.loop(0, CX)
    def _(x):
        uv[x] = vp[x + 1] * flow[x]
    plate_row = iota((128, 128), 0)
    hots = [jnp.where(plates_ref[q:q + 1, :] == plate_row, 1.0, 0.0).astype(BF16) for q in range(4)]
    hot = jnp.concatenate(hots, axis=1)
    flat = uv.reshape(CX * CY, CZ)
    pflat = part.reshape(128 * 8, CZ)
    for j in range(8):
        u = flat[pl.ds(j, 512, stride=8), :]
        hi = u.astype(BF16)
        lo = (u - hi.astype(F32)).astype(BF16)
        pflat[pl.ds(j, 128, stride=8), :] = (
            jnp.dot(hot, hi, preferred_element_type=F32) + jnp.dot(hot, lo, preferred_element_type=F32))
    stage_a = []
    for k in range(1, NCAP):
        to = lax.rem(cap + k, NCAP)
        cp = rcopy(part.at[pl.ds(to * 32, 32)], recv_a.at[k], pas.at[k], par.at[k], cap=to)
        cp.start()
        stage_a.append(cp)

    mine_k = pl.ds(pl.multiple_of(rad * HALF, HALF), HALF)
    dampc[...] = jnp.broadcast_to(damp_ref[:, mine_k], (CZ, HALF)).T

    basis_cp.wait()
    krow = rad * HALF
    swaps, stage_b = [], []

    def source_of(dx, dz):
        return lax.rem(mx + 4 - dx, 4) * 4 + lax.rem(mz + 4 - dz, 4)

    def receive(batch):
        for dx, dz in batch:
            if dx or dz:
                src = source_of(dx, dz)
                k = dx * 4 + dz
                rcopy(fb.at[src], xm.at[src], as_.at[k], ar_.at[k], lat=src).wait_recv()
                forward(src).start()

    def terms(batch):
        for dx, dz in batch:
            forward(source_of(dx, dz)).wait_recv()
        runs = [(lax.rem(mx + 4 - batch[0][0], 4) * 4, 4)] if len(batch) == 4 else [(source_of(*o), 1) for o in batch]
        out = []
        for at, n in runs:
            cols = pl.ds(pl.multiple_of(at * CY, CY), n * CY)
            halves = [ref[pl.ds(at, n)].reshape(n * CY, CZ) for ref in (xm, xo)]
            out.append((cols, jnp.concatenate(halves, axis=1)))
        return out

    def product(parts, i):
        krows = pl.ds(pl.multiple_of(krow + i * 1024, 1024), 1024)
        total = None
        for cols, xs in parts:
            prod = jnp.dot(basis[krows, cols], xs, preferred_element_type=F32)
            total = prod if total is None else total + prod
        return total

    batches = [[(1, 2), (1, 1), (1, 3), (1, 0)], [(3, 2), (3, 1), (3, 3), (3, 0)],
               [(0, 0), (2, 2), (0, 1), (2, 1), (0, 3)], [(2, 3), (0, 2), (2, 0)]]
    for step, batch in enumerate(batches):
        if step == 0:
            receive(batch)
            receive(batches[1])
        elif step == 2:
            receive(batch)
        parts = terms(batch)
        if step == 2:
            receive(batches[3])
        for i in range(2):
            crow = slice(i * 1024, (i + 1) * 1024)
            prod = product(parts, i)
            if step == 0:
                coef[crow, :] = prod
            elif step < 3:
                coef[crow, :] += prod
            else:
                whole = coef[crow, :] + prod
                krows = pl.ds(pl.multiple_of(krow + i * 1024, 1024), 1024)
                dcol = dampc[crow, :]
                st[1, :, krows] = (whole[:, CZ:] * dcol).astype(BF16).T
                swaps.append(rcopy(st.at[1, :, krows], st.at[0, :, krows], ss.at[i], sr.at[i], rad=sib))
                swaps[i].start()
                st[0, :, krows] = (whole[:, :CZ] * dcol).astype(BF16).T
        if step == 1:
            for cp in stage_a:
                cp.wait()
            acc_a[...] = (part[pl.ds(cap * 32, 32)] + recv_a[1] + recv_a[2] + recv_a[3])
            recv_b[lat] = acc_a[pl.ds(lat * 2, 2)]
            for k in range(1, NLAT):
                to = lax.rem(lat + k, NLAT)
                cp = rcopy(acc_a.at[pl.ds(to * 2, 2)], recv_b.at[lat], pbs.at[k], pbr.at[k], lat=to)
                cp.start()
                stage_b.append(cp)

    for cp in stage_b:
        cp.wait()
    acc_b[...] = jnp.sum(recv_b[...], axis=0)
    swap_c = rcopy(acc_b.at[sib], recv_c, pcs, pcr, rad=sib)
    swap_c.start()

    def ship(res, first):
        outb[pl.ds(first, 2)] = res.T.astype(BF16).reshape(2, CY, CZ)

    def home(dest):
        return rcopy(outb.at[dest], rec.at[lat], rs.at[dest], rr.at[lat], lat=dest)

    def chunk(first):
        return pl.ds(pl.multiple_of(first * CY, 512), 512)

    near = pl.ds(pl.multiple_of(rad * HALF, HALF), HALF)
    far = pl.ds(pl.multiple_of(sib * HALF, HALF), HALF)
    for n, (dx, half) in enumerate([(1, 0), (3, 1), (1, 1), (3, 0), (2, 0), (0, 1), (2, 1), (0, 0)]):
        first = lax.rem(mx + dx, 4) * 4 + 2 * half
        if n == 0:
            res = jnp.dot(st[0, :, near], basis[near, chunk(first)], preferred_element_type=F32)
            for cp in swaps:
                cp.wait()
            res += jnp.dot(st[0, :, far], basis[far, chunk(first)], preferred_element_type=F32)
        else:
            res = jnp.dot(st[0], basis[:, chunk(first)], preferred_element_type=F32)
        ship(res, first)
        for q in range(2):
            if dx:
                home(first + q).start()
            else:
                @pl.when(first + q != lat)
                def _():
                    home(first + q).start()

    uv[lat] = flow[lat] + outb[lat].astype(F32)
    swap_c.wait()
    tect_ref[rad] = acc_b[rad]
    tect_ref[sib] = recv_c[...]
    pltpu.make_async_copy(arrived, arrived, g_send).wait()
    for dx, dz in steps:
        carry_out(dx, dz).wait_send()
    for src in range(NLAT):
        forward(src).wait_send()
    for dx, dz in [(1, 0), (1, 1), (3, 2), (3, 3), (1, 2), (1, 3), (3, 0), (3, 1), (2, 0), (2, 1), (0, 2), (0, 3), (2, 2), (2, 3), (0, 1)]:
        src = lax.rem(mx + 4 - dx, 4) * 4 + lax.rem(mz + dz, 4)
        rcopy(outb.at[src], rec.at[src], rs.at[src], rr.at[src], lat=src).wait_recv()
        uv[src] = flow[src] + rec[src].astype(F32)
    for dx, dz in steps:
        home(away(dx, dz)).wait_send()


def finish(flow, thermal, tect, flow_out, thermal_out, tect_out, sem):
    copies = [pltpu.make_async_copy(flow, flow_out, sem.at[0]), pltpu.make_async_copy(thermal, thermal_out, sem.at[1])]
    for cp in copies:
        cp.start()
    for r in range(2):
        for j in range(8):
            tect_out[0, r:r + 1, j * CZ:(j + 1) * CZ] = tect[r, j:j + 1, :]
    for cp in copies:
        cp.wait()


def body(forcing, viscosity, harmonic_basis, damping_weights, unit_plates):
    DMA = pltpu.SemaphoreType.DMA
    vm = pltpu.VMEM
    anys = pl.BlockSpec(memory_space=pl.ANY)
    vmem = pl.BlockSpec(memory_space=pltpu.VMEM)
    block = (CX, CY, CZ)
    tile = (CX, 8, CZ)
    face = (CY, CZ)
    flow, thermal, tect = pl.pallas_call(
        kernel,
        out_shape=(vm(block, F32), vm(block, F32), vm((2, 8, CZ), F32)),
        in_specs=[anys, anys, anys, vmem, vmem],
        out_specs=(vmem, vmem, vmem),
        scratch_shapes=[
            vm((18, CY, CZ), F32), vm((18, CY, CZ), F32), vm(block, F32), vm(block, F32), vm(block, BF16),
            vm((NY, NY), BF16), vm(block, BF16), vm(block, BF16), vm((HALF, 256), F32), vm((HALF, CZ), F32),
            vm((2, CZ, NY), BF16), vm(block, BF16), vm(block, BF16),
            vm(face, F32), vm(face, F32), vm(face, F32), vm(face, F32), vm(face, F32), vm(face, F32),
            vm(tile, F32), vm(tile, F32), vm(tile, F32), vm(tile, F32), vm(tile, F32),
            vm((CY // 2, CZ), F32), vm((CY // 2, CZ), F32),
            vm((128, 8, CZ), F32), vm((4, 32, 8, CZ), F32), vm((32, 8, CZ), F32),
            vm((NLAT, 2, 8, CZ), F32), vm((2, 8, CZ), F32), vm((8, CZ), F32),
            vm((1, CZ), F32), vm((128, 1, CZ), F32),
            DMA((2,)), DMA, pltpu.SemaphoreType.REGULAR, DMA((14,)), DMA((14,)), DMA, DMA,
            DMA((16,)), DMA((16,)), DMA((16,)), DMA((16,)), DMA((2,)), DMA((2,)), DMA((16,)), DMA((16,)),
            DMA((4,)), DMA((4,)), DMA((16,)), DMA((16,)), DMA, DMA,
        ],
        compiler_params=pltpu.CompilerParams(
            vmem_limit_bytes=56 << 20, collective_id=0, has_side_effects=True),
        name="adjoint",
    )(forcing, viscosity, harmonic_basis, damping_weights.reshape(1, NY), unit_plates.reshape(4, 128))
    return pl.pallas_call(
        finish,
        out_shape=(
            jax.ShapeDtypeStruct(block, F32),
            jax.ShapeDtypeStruct(block, F32),
            jax.ShapeDtypeStruct((1, 2, 8 * CZ), F32),
        ),
        in_specs=[vmem, vmem, vmem],
        out_specs=(anys, anys, vmem),
        scratch_shapes=[DMA((2,))],
        compiler_params=pltpu.CompilerParams(vmem_limit_bytes=16 << 20),
        name="finish",
    )(flow, thermal, tect)


def solution(mesh):
    in_specs = (
        P("cap", "lat", "rad"),
        P("cap", "lat", "rad"),
        P(),
        P(),
        P(("cap", "lat"), None, None),
    )
    out_specs = (
        P("cap", "lat", "rad"),
        P("cap", "lat", "rad"),
        P(("cap", "lat", "rad"), None, None),
    )
    return jax.shard_map(body, mesh=mesh, in_specs=in_specs, out_specs=out_specs, check_vma=False)
```

```python
import jax
import jax.numpy as jnp
from jax import lax
from jax.experimental import pallas as pl
from jax.experimental.pallas import tpu as pltpu
from jax.sharding import PartitionSpec as P

MESH = pl.DeviceIdType.MESH
F32 = jnp.float32
BF16 = jnp.bfloat16
CX, CY, CZ = 16, 256, 128
NY = 4096
RB = 64
NB = CY // RB
NLAT, NCAP, NRAD = 16, 4, 2
HALF = NY // 2


def iota(shape, dim):
    return lax.broadcasted_iota(jnp.int32, shape, dim)


def fold(x):
    return jnp.sum(x.reshape(x.shape[0] // 8, 8, CZ), axis=0)


def kernel(b_hbm, v_hbm, basis_hbm, damp_ref, plates_ref, flow, uv, tect_ref,
           bp, vp, vy, vz, fb, basis, xm, xo, coef, dampc, st, outb, rec,
           pb, pv, pu, qb, qv, qu, ybm, ybp, yvm, yvp, yu, xup, xdn,
           part, recv_a, acc_a, recv_b, acc_b, recv_c, mine, rows,
           loc_sem, basis_sem, deep, hs, hr, g_send, g_recv,
           as_, ar_, fs, fr, ss, sr, rs, rr, pas, par, pbs, pbr, pcs, pcr):
    cap = lax.axis_index("cap")
    lat = lax.axis_index("lat")
    rad = lax.axis_index("rad")
    mx = lat // 4
    mz = lax.rem(lat, 4)
    up_cap, dn_cap = lax.rem(cap + 1, NCAP), lax.rem(cap + NCAP - 1, NCAP)
    up_lat, dn_lat = lax.rem(lat + 1, NLAT), lax.rem(lat + NLAT - 1, NLAT)
    sib = 1 - rad

    loads = [
        pltpu.make_async_copy(b_hbm, bp.at[1:17], loc_sem.at[0]),
        pltpu.make_async_copy(v_hbm, vp.at[1:17], loc_sem.at[1]),
    ]
    for cp in loads:
        cp.start()

    bar = pltpu.get_barrier_semaphore()
    column = [(k // 2, k % 2) for k in range(1, 8)]

    def tell(sem, **dev):
        pl.semaphore_signal(sem, inc=1, device_id=dev, device_id_type=MESH)

    def fellow(k):
        return {"cap": lax.rem(cap + k[0], NCAP), "rad": lax.rem(rad + k[1], NRAD)}

    for k in column:
        tell(bar, **fellow(k))
    for k in range(1, NLAT):
        tell(bar, lat=lax.rem(lat + k, NLAT))
    pl.semaphore_wait(bar, 22)

    def rcopy(src, dst, ssem, rsem, **dev):
        return pltpu.make_async_remote_copy(
            src_ref=src, dst_ref=dst, send_sem=ssem, recv_sem=rsem, device_id=dev, device_id_type=MESH)

    yh, xh = [], []
    for q, (hbm, pad, lo, hi) in enumerate(((b_hbm, bp, ybm, ybp), (v_hbm, vp, yvm, yvp))):
        yh.append(rcopy(hbm.at[:, 248:256, :], lo, hs.at[q], hr.at[q], lat=up_lat))
        yh.append(rcopy(hbm.at[:, 0:8, :], hi, hs.at[2 + q], hr.at[2 + q], lat=dn_lat))
        xh.append(rcopy(hbm.at[15], pad.at[0], hs.at[4 + q], hr.at[4 + q], cap=up_cap))
        xh.append(rcopy(hbm.at[0], pad.at[17], hs.at[6 + q], hr.at[6 + q], cap=dn_cap))
    for cp in xh + yh:
        cp.start()
    for cp in loads:
        cp.wait()
    lane = iota((RB, CZ), 1)
    row = iota((RB, CZ), 0)
    edge = (lane == 0) | (lane == CZ - 1)

    def pack(ref, base, dst):
        for yb in range(NB):
            rows_ = slice(yb * RB, (yb + 1) * RB)
            acc = jnp.zeros((RB, CZ), F32)
            for x in range(CX):
                acc = jnp.where(lane // 2 == x, pltpu.roll(ref[base + x, rows_, :], 2 * x + 1, 1), acc)
            dst[rows_, :] = acc

    wide = iota((CY, CZ), 1)
    facing = lax.rem(wide, 2) == rad

    def across(q):
        turned = jnp.where(rad == 0, pltpu.roll(q, CZ - 1, 1), pltpu.roll(q, 1, 1))
        return jnp.where(facing, turned, 0.0)

    pack(bp, 1, pb)
    zb = rcopy(pb, qb, hs.at[8], hr.at[8], rad=sib)
    zb.start()
    pack(vp, 1, pv)
    zv = rcopy(pv, qv, hs.at[9], hr.at[9], rad=sib)
    zv.start()
    for k in column:
        tell(deep, **fellow(k))
    basis_cp = pltpu.make_async_copy(basis_hbm, basis, basis_sem)
    basis_cp.start()
    zero = jnp.zeros((8, CZ), F32)

    def square(x, s):
        b0 = bp[x]
        return s + jnp.sum((b0 * b0).reshape(4, 8, 8, CZ), axis=1)

    m0 = jnp.sum(lax.fori_loop(1, 17, square, jnp.zeros((4, 8, CZ), F32)), axis=0)
    zb.wait()
    zv.wait()
    qv[...] = pv[...] + across(qv[...])
    qb[...] = qv[...] * (pb[...] - across(qb[...]))

    def plane(X, carry):
        shift = CZ + 1 - 2 * X
        before = jnp.zeros((1, CZ), F32)
        for yb in range(NB):
            y0 = yb * RB
            rows_ = slice(y0, y0 + RB)
            b0, v0 = bp[X, rows_, :], vp[X, rows_, :]
            acc = (v0 + vp[X + 1, rows_, :]) * (b0 - bp[X + 1, rows_, :])
            acc += (v0 + vp[X - 1, rows_, :]) * (b0 - bp[X - 1, rows_, :])
            if yb < NB - 1:
                near = slice(y0 + 1, y0 + 1 + RB)
                pair = v0 + vp[X, near, :]
                flux = pair * (b0 - bp[X, near, :])
            else:
                pair = jnp.where(row < RB - 1, v0 + pltpu.roll(v0, RB - 1, 0), 0.0)
                flux = pair * (b0 - pltpu.roll(b0, RB - 1, 0))
            vy[X - 1, rows_, :] = pair
            acc += flux - jnp.where(row > 0, pltpu.roll(flux, 1, 0), before)
            before = flux[RB - 1:RB, :]
            pair = jnp.where(lane < CZ - 1, v0 + pltpu.roll(v0, CZ - 1, 1), 0.0)
            vz[X - 1, rows_, :] = pair
            flux = pair * (b0 - pltpu.roll(b0, CZ - 1, 1))
            acc += flux - pltpu.roll(flux, 1, 1)
            acc += jnp.where(edge, pltpu.roll(qb[rows_, :], shift, 1), 0.0)
            uv[X - 1, rows_, :] = acc
        return carry

    low_y = jnp.where(lat == 0, 0.0, 1.0).astype(F32)
    high_y = jnp.where(lat == NLAT - 1, 0.0, 1.0).astype(F32)

    def lat_faces(a, b):
        for at, bh, vh, far, keep in ((0, ybm, yvm, 7, low_y), (255, ybp, yvp, 0, high_y)):
            here = slice(at, at + 1)
            there = slice(far, far + 1)
            uv[a:b, here, :] += ((vp[a + 1:b + 1, here, :] + keep * vh[a:b, there, :])
                                 * (bp[a + 1:b + 1, here, :] - keep * bh[a:b, there, :]))

    def energy(x, sums, with_x):
        n1, n2, n3 = sums
        for yb in range(NB):
            y0 = yb * RB
            rows_ = slice(y0, y0 + RB)
            u0, b0 = uv[x, rows_, :], bp[x + 1, rows_, :]
            d = u0 - pltpu.roll(u0, CZ - 1, 1)
            acc = vz[x, rows_, :] * (d * d)
            if with_x:
                d = u0 - uv[x + 1, rows_, :]
                acc += (vp[x + 1, rows_, :] + vp[x + 2, rows_, :]) * (d * d)
            if yb < NB - 1:
                d = u0 - uv[x, y0 + 1:y0 + 1 + RB, :]
            else:
                d = u0 - pltpu.roll(u0, RB - 1, 0)
            acc += vy[x, rows_, :] * (d * d)
            n1 += fold(b0 * u0)
            n2 += fold(u0 * u0)
            n3 += fold(acc)
        return n1, n2, n3

    lax.fori_loop(2, 16, plane, 0)
    for cp in yh:
        cp.wait()
    lat_faces(1, 15)
    for cp in xh:
        cp.wait()
    for side, at in ((0, 0), (NCAP - 1, 17)):
        @pl.when(cap == side)
        def _():
            bp[at] = jnp.zeros((CY, CZ), F32)
            vp[at] = jnp.zeros((CY, CZ), F32)
    plane(1, 0)
    plane(16, 0)
    lat_faces(0, 1)
    lat_faces(15, 16)

    mid = CY // 2
    ux = [
        rcopy(uv.at[0, 0:mid], xup, hs.at[10], hr.at[10], cap=dn_cap),
        rcopy(uv.at[15, mid:CY], xdn, hs.at[11], hr.at[11], cap=up_cap),
    ]
    for cp in ux:
        cp.start()
    uy = rcopy(uv.at[:, 0:8, :], yu, hs.at[12], hr.at[12], lat=dn_lat)
    uy.start()
    pack(uv, 0, pu)
    uz = rcopy(pu, qu, hs.at[13], hr.at[13], rad=sib)
    uz.start()
    sums = lax.fori_loop(0, 15, lambda x, s: energy(x, s, True), (zero, zero, zero))
    n1, n2, n3 = energy(15, sums, False)
    u0, u15 = uv[0, 0:mid], uv[15, mid:CY]
    first = jnp.where(cap == 0, 1.0, 0.0).astype(F32)
    last = jnp.where(cap == NCAP - 1, 1.0, 0.0).astype(F32)
    n3 += fold(first * vp[1, 0:mid] * (u0 * u0)) + fold(last * vp[16, mid:CY] * (u15 * u15))
    u0 = uv[:, 0:1, :]
    edge_row = jnp.sum((1.0 - low_y) * vp[1:17, 0:1, :] * (u0 * u0), axis=0)
    uz.wait()
    d = pu[...] - across(qu[...])
    n3 += fold(jnp.where(facing, 0.5, 1.0) * qv[...] * (d * d))
    uy.wait()
    d = uv[:, 255:256, :] - high_y * yu[:, 0:1, :]
    edge_row += jnp.sum((vp[1:17, 255:256, :] + high_y * yvp[:, 0:1, :]) * (d * d), axis=0)
    for cp in ux:
        cp.wait()
    d = uv[15, 0:mid] - (1.0 - last) * xup[...]
    n3 += fold((vp[16, 0:mid] + vp[17, 0:mid]) * (d * d))
    d = uv[0, mid:CY] - (1.0 - first) * xdn[...]
    n3 += fold((vp[1, mid:CY] + vp[0, mid:CY]) * (d * d))

    lane1 = iota((1, CZ), 1)
    line = jnp.zeros((1, CZ), F32)
    for q, s in enumerate((m0, n1, n2, n3)):
        s = jnp.sum(s, axis=0, keepdims=True)
        if q == 3:
            s = s + edge_row
        line = jnp.where(lane1 == q, jnp.sum(s, axis=1, keepdims=True), line)
    mine[...] = line
    place = (cap * NLAT + lat) * NRAD + rad
    rows[place] = line
    pl.semaphore_wait(deep, 7)
    ring = (0, 1, 2, 1)
    others = sorted(((c, x, z, r) for c in range(4) for x in range(4) for z in range(4) for r in range(2)),
                    key=lambda o: -(ring[o[0]] + ring[o[1]] + ring[o[2]]))
    for c, x, z, r in others:
        if (c, x, z, r) != (0, 0, 0, 0):
            rcopy(mine, rows.at[place], g_send, g_recv,
                  cap=lax.rem(cap + c, NCAP), lat=lax.rem(mx + x, 4) * 4 + lax.rem(mz + z, 4),
                  rad=lax.rem(rad + r, NRAD)).start()
    arrived = rows.at[pl.ds(0, 127)]
    pltpu.make_async_copy(arrived, arrived, g_recv).wait()
    tot = jnp.sum(rows[...], axis=0)
    t0, e1, e2, e3 = [jnp.sum(jnp.where(lane1 == q, tot, 0.0), axis=1, keepdims=True) for q in range(4)]
    e1, e2, e3 = 0.5 * e1 / t0, 0.25 * e2 / t0, 0.125 * e3 / t0
    step0 = 1.0 / (1.0 + e1)
    ratio = jnp.maximum((e2 - e1 * e1) * step0 * step0, 0.0)
    g, h = (1.0 - step0) + ratio, -step0
    pap = g * g * (1.0 + e1) + 2.0 * g * h * (e1 + e2) + h * h * (e2 + e3)
    step1 = ratio / jnp.maximum(jnp.maximum(pap, ratio), 1e-30)
    alpha, beta = step0 + step1 * g, 0.5 * step1 * h

    def away(dx, dz):
        return lax.rem(mx + dx, 4) * 4 + lax.rem(mz + dz, 4)

    def solve(x):
        f = alpha * bp[x + 1] + beta * uv[x]
        flow[x] = f
        fb[x] = f.astype(BF16)

    steps = [(1, 2), (3, 0), (1, 1), (3, 3), (1, 3), (3, 1), (1, 0), (3, 2), (2, 2), (0, 1), (2, 1), (0, 3), (2, 3), (0, 2), (2, 0)]

    def carry_out(dx, dz):
        dest = away(dx, dz)
        k = dx * 4 + dz
        return rcopy(fb.at[dest], xm.at[lat], as_.at[k], ar_.at[k], lat=dest)

    for dx, dz in steps:
        solve(away(dx, dz))
        carry_out(dx, dz).start()
    solve(lat)
    xm[lat] = fb[lat]

    def forward(src):
        return rcopy(xm.at[src], xo.at[src], fs.at[src], fr.at[src], rad=sib)

    forward(lat).start()

    @pl.loop(0, CX)
    def _(x):
        uv[x] = vp[x + 1] * flow[x]
    plate_row = iota((128, 128), 0)
    hots = [jnp.where(plates_ref[q:q + 1, :] == plate_row, 1.0, 0.0).astype(BF16) for q in range(4)]
    hot = jnp.concatenate(hots, axis=1)
    flat = uv.reshape(CX * CY, CZ)
    pflat = part.reshape(128 * 8, CZ)
    for j in range(8):
        u = flat[pl.ds(j, 512, stride=8), :]
        hi = u.astype(BF16)
        lo = (u - hi.astype(F32)).astype(BF16)
        pflat[pl.ds(j, 128, stride=8), :] = (
            jnp.dot(hot, hi, preferred_element_type=F32) + jnp.dot(hot, lo, preferred_element_type=F32))
    stage_a = []
    for k in range(1, NCAP):
        to = lax.rem(cap + k, NCAP)
        cp = rcopy(part.at[pl.ds(to * 32, 32)], recv_a.at[k], pas.at[k], par.at[k], cap=to)
        cp.start()
        stage_a.append(cp)

    mine_k = pl.ds(pl.multiple_of(rad * HALF, HALF), HALF)
    dampc[...] = jnp.broadcast_to(damp_ref[:, mine_k], (CZ, HALF)).T

    basis_cp.wait()
    krow = rad * HALF
    swaps, stage_b = [], []

    def source_of(dx, dz):
        return lax.rem(mx + 4 - dx, 4) * 4 + lax.rem(mz + 4 - dz, 4)

    def receive(batch):
        for dx, dz in batch:
            if dx or dz:
                src = source_of(dx, dz)
                k = dx * 4 + dz
                rcopy(fb.at[src], xm.at[src], as_.at[k], ar_.at[k], lat=src).wait_recv()
                forward(src).start()

    def terms(batch):
        for dx, dz in batch:
            forward(source_of(dx, dz)).wait_recv()
        runs = [(lax.rem(mx + 4 - batch[0][0], 4) * 4, 4)] if len(batch) == 4 else [(source_of(*o), 1) for o in batch]
        out = []
        for at, n in runs:
            cols = pl.ds(pl.multiple_of(at * CY, CY), n * CY)
            halves = [ref[pl.ds(at, n)].reshape(n * CY, CZ) for ref in (xm, xo)]
            out.append((cols, jnp.concatenate(halves, axis=1)))
        return out

    def product(parts, i):
        krows = pl.ds(pl.multiple_of(krow + i * 1024, 1024), 1024)
        total = None
        for cols, xs in parts:
            prod = jnp.dot(basis[krows, cols], xs, preferred_element_type=F32)
            total = prod if total is None else total + prod
        return total

    batches = [[(1, 2), (1, 1), (1, 3), (1, 0)], [(3, 0), (3, 3), (3, 1), (3, 2)],
               [(0, 0), (2, 2), (0, 1), (2, 1), (0, 3)], [(2, 3), (0, 2), (2, 0)]]
    for step, batch in enumerate(batches):
        if step == 0:
            receive(batch)
            receive(batches[1])
        elif step == 2:
            receive(batch)
        parts = terms(batch)
        if step == 2:
            receive(batches[3])
        for i in range(2):
            crow = slice(i * 1024, (i + 1) * 1024)
            prod = product(parts, i)
            if step == 0:
                coef[crow, :] = prod
            elif step < 3:
                coef[crow, :] += prod
            else:
                whole = coef[crow, :] + prod
                krows = pl.ds(pl.multiple_of(krow + i * 1024, 1024), 1024)
                dcol = dampc[crow, :]
                st[1, :, krows] = (whole[:, CZ:] * dcol).astype(BF16).T
                swaps.append(rcopy(st.at[1, :, krows], st.at[0, :, krows], ss.at[i], sr.at[i], rad=sib))
                swaps[i].start()
                st[0, :, krows] = (whole[:, :CZ] * dcol).astype(BF16).T
        if step == 1:
            for cp in stage_a:
                cp.wait()
            acc_a[...] = (part[pl.ds(cap * 32, 32)] + recv_a[1] + recv_a[2] + recv_a[3])
            recv_b[lat] = acc_a[pl.ds(lat * 2, 2)]
            for k in range(1, NLAT):
                to = lax.rem(lat + k, NLAT)
                cp = rcopy(acc_a.at[pl.ds(to * 2, 2)], recv_b.at[lat], pbs.at[k], pbr.at[k], lat=to)
                cp.start()
                stage_b.append(cp)

    for cp in stage_b:
        cp.wait()
    acc_b[...] = jnp.sum(recv_b[...], axis=0)
    swap_c = rcopy(acc_b.at[sib], recv_c, pcs, pcr, rad=sib)
    swap_c.start()

    def ship(res, first):
        outb[pl.ds(first, 2)] = res.T.astype(BF16).reshape(2, CY, CZ)

    def home(dest):
        return rcopy(outb.at[dest], rec.at[lat], rs.at[dest], rr.at[lat], lat=dest)

    def chunk(first):
        return pl.ds(pl.multiple_of(first * CY, 512), 512)

    near = pl.ds(pl.multiple_of(rad * HALF, HALF), HALF)
    far = pl.ds(pl.multiple_of(sib * HALF, HALF), HALF)
    for n, (dx, half) in enumerate([(1, 0), (3, 1), (1, 1), (3, 0), (2, 0), (0, 1), (2, 1), (0, 0)]):
        first = lax.rem(mx + dx, 4) * 4 + 2 * half
        if n == 0:
            res = jnp.dot(st[0, :, near], basis[near, chunk(first)], preferred_element_type=F32)
            for cp in swaps:
                cp.wait()
            res += jnp.dot(st[0, :, far], basis[far, chunk(first)], preferred_element_type=F32)
        else:
            res = jnp.dot(st[0], basis[:, chunk(first)], preferred_element_type=F32)
        ship(res, first)
        for q in range(2):
            if dx:
                home(first + q).start()
            else:
                @pl.when(first + q != lat)
                def _():
                    home(first + q).start()

    uv[lat] = flow[lat] + outb[lat].astype(F32)
    swap_c.wait()
    tect_ref[rad] = acc_b[rad]
    tect_ref[sib] = recv_c[...]
    pltpu.make_async_copy(arrived, arrived, g_send).wait()
    for dx, dz in steps:
        carry_out(dx, dz).wait_send()
    for src in range(NLAT):
        forward(src).wait_send()
    for dx, dz in [(1, 0), (1, 1), (3, 2), (3, 3), (1, 2), (1, 3), (3, 0), (3, 1), (2, 0), (2, 1), (0, 2), (0, 3), (2, 2), (2, 3), (0, 1)]:
        src = lax.rem(mx + 4 - dx, 4) * 4 + lax.rem(mz + dz, 4)
        rcopy(outb.at[src], rec.at[src], rs.at[src], rr.at[src], lat=src).wait_recv()
        uv[src] = flow[src] + rec[src].astype(F32)
    for dx, dz in steps:
        home(away(dx, dz)).wait_send()


def finish(flow, thermal, tect, flow_out, thermal_out, tect_out, sem):
    copies = [pltpu.make_async_copy(flow, flow_out, sem.at[0]), pltpu.make_async_copy(thermal, thermal_out, sem.at[1])]
    for cp in copies:
        cp.start()
    for r in range(2):
        for j in range(8):
            tect_out[0, r:r + 1, j * CZ:(j + 1) * CZ] = tect[r, j:j + 1, :]
    for cp in copies:
        cp.wait()


def body(forcing, viscosity, harmonic_basis, damping_weights, unit_plates):
    DMA = pltpu.SemaphoreType.DMA
    vm = pltpu.VMEM
    anys = pl.BlockSpec(memory_space=pl.ANY)
    vmem = pl.BlockSpec(memory_space=pltpu.VMEM)
    block = (CX, CY, CZ)
    tile = (CX, 8, CZ)
    face = (CY, CZ)
    flow, thermal, tect = pl.pallas_call(
        kernel,
        out_shape=(vm(block, F32), vm(block, F32), vm((2, 8, CZ), F32)),
        in_specs=[anys, anys, anys, vmem, vmem],
        out_specs=(vmem, vmem, vmem),
        scratch_shapes=[
            vm((18, CY, CZ), F32), vm((18, CY, CZ), F32), vm(block, F32), vm(block, F32), vm(block, BF16),
            vm((NY, NY), BF16), vm(block, BF16), vm(block, BF16), vm((HALF, 256), F32), vm((HALF, CZ), F32),
            vm((2, CZ, NY), BF16), vm(block, BF16), vm(block, BF16),
            vm(face, F32), vm(face, F32), vm(face, F32), vm(face, F32), vm(face, F32), vm(face, F32),
            vm(tile, F32), vm(tile, F32), vm(tile, F32), vm(tile, F32), vm(tile, F32),
            vm((CY // 2, CZ), F32), vm((CY // 2, CZ), F32),
            vm((128, 8, CZ), F32), vm((4, 32, 8, CZ), F32), vm((32, 8, CZ), F32),
            vm((NLAT, 2, 8, CZ), F32), vm((2, 8, CZ), F32), vm((8, CZ), F32),
            vm((1, CZ), F32), vm((128, 1, CZ), F32),
            DMA((2,)), DMA, pltpu.SemaphoreType.REGULAR, DMA((14,)), DMA((14,)), DMA, DMA,
            DMA((16,)), DMA((16,)), DMA((16,)), DMA((16,)), DMA((2,)), DMA((2,)), DMA((16,)), DMA((16,)),
            DMA((4,)), DMA((4,)), DMA((16,)), DMA((16,)), DMA, DMA,
        ],
        compiler_params=pltpu.CompilerParams(
            vmem_limit_bytes=56 << 20, collective_id=0, has_side_effects=True),
        name="adjoint",
    )(forcing, viscosity, harmonic_basis, damping_weights.reshape(1, NY), unit_plates.reshape(4, 128))
    return pl.pallas_call(
        finish,
        out_shape=(
            jax.ShapeDtypeStruct(block, F32),
            jax.ShapeDtypeStruct(block, F32),
            jax.ShapeDtypeStruct((1, 2, 8 * CZ), F32),
        ),
        in_specs=[vmem, vmem, vmem],
        out_specs=(anys, anys, vmem),
        scratch_shapes=[DMA((2,))],
        compiler_params=pltpu.CompilerParams(vmem_limit_bytes=16 << 20),
        name="finish",
    )(flow, thermal, tect)


def solution(mesh):
    in_specs = (
        P("cap", "lat", "rad"),
        P("cap", "lat", "rad"),
        P(),
        P(),
        P(("cap", "lat"), None, None),
    )
    out_specs = (
        P("cap", "lat", "rad"),
        P("cap", "lat", "rad"),
        P(("cap", "lat", "rad"), None, None),
    )
    return jax.shard_map(body, mesh=mesh, in_specs=in_specs, out_specs=out_specs, check_vma=False)
```
